32 devices in a mesh: ctx: 8 (over y, x, core), tp: 4 (over z).
Axes of the slice: x: 2, y: 2, z: 4, core: 2. Of those that a mesh axis runs over, the one named last changes fastest.
Arguments:
- query_proj: bfloat16 [16384, 1024], P(('ctx', 'tp')), may hold values from -6 to 6
- key_proj: bfloat16 [16384, 1024], P(('ctx', 'tp')), may hold values from -6 to 6
- value_proj: bfloat16 [16384, 1024], P(('ctx', 'tp')), may hold values from -6 to 6
- long_filter: float32 [16384, 1024], P('ctx', 'tp'), may hold values from 0 to 0.4
- short_filter: float32 [3, 3, 1024], P(None, None, 'tp'), may hold values from -3 to 3
- skip_bias: float32 [1024], P('tp'), may hold values from 0.5 to 1.5
Outputs:
- gated_output: float32 [16384, 1024], P(('ctx', 'tp'))
The draws below stay inside these ranges and needn't reach their ends.
All inputs are finite; a program needn't handle non-finite values.
Results may differ from the reference program's by a relative error of at most 0.0003.
Values may be sent and summed in bfloat16 or wider, within the bound.
No kernel may reach another device: no remote copies, remote signals or barrier semaphores. Data moves between devices by JAX's collectives and lax.ppermute only.
A program may use at most 128 MiB of HBM per device.

```python
import math
import jax
import jax.numpy as jnp
from jax import lax

FEATURE_WIDTH = 1024
SEQUENCE_LENGTH = 16384


def draw_long_filter(key, part):
    random_seeds = jax.random.split(key, 4)
    lowest = math.log(30.0)
    upper_log = math.log(64.0 * SEQUENCE_LENGTH)
    lifetime = jnp.exp(jax.random.uniform(random_seeds[0], (1, FEATURE_WIDTH), jnp.float32, lowest, upper_log))
    element_offset = jnp.arange(SEQUENCE_LENGTH, dtype=jnp.int32)[:, None]
    kernel_magnitude = jnp.sqrt(jnp.expm1(-2.0 / lifetime) / jnp.expm1(-2.0 * SEQUENCE_LENGTH / lifetime))
    kernel_jaggedness = jax.random.uniform(random_seeds[1], (SEQUENCE_LENGTH, FEATURE_WIDTH), jnp.float32, 0.5, 1.5)
    spike_locations = jax.random.randint(random_seeds[2], (4, FEATURE_WIDTH), 0, SEQUENCE_LENGTH)
    length_divisors = jax.random.uniform(random_seeds[3], (4, FEATURE_WIDTH), jnp.float32, 0.5, 0.8)
    kernel_spikes = jnp.ones((SEQUENCE_LENGTH, FEATURE_WIDTH), jnp.float32)
    for element_ordinal in range(4):
        kernel_spikes = kernel_spikes * jnp.where(element_offset >= spike_locations[element_ordinal][None, :], length_divisors[element_ordinal][None, :], 1.0)
    falloff_speed = jnp.exp(-element_offset.astype(jnp.float32) / lifetime)
    return kernel_magnitude * falloff_speed * kernel_jaggedness * kernel_spikes


def block_levels(stream_key, dims, pieces, least, largest):
    factor_of, own = 1.0, jax.random.fold_in(stream_key, 6)
    for dim, shards_of in pieces:
        draws = jnp.exp(jax.random.uniform(jax.random.fold_in(own, dim), (shards_of,), jnp.float32, least / len(pieces), largest / len(pieces)))
        factor_of = factor_of * jnp.repeat(draws, dims[dim] // shards_of).reshape([-1 if axis == dim else 1 for axis in range(len(dims))])
    return factor_of


def gaussian(key, extent, scale, bound, shards=(), held_as=jnp.bfloat16):
    level = block_levels(key, extent, shards, -0.22, 0.18) if shards else 1.0
    array = jax.random.normal(key, extent, jnp.float32) * scale * level
    return jnp.minimum(jnp.maximum(array, -bound), bound).astype(held_as)


def setup_inputs(seed: int = 0) -> dict:
    splits = jax.random.split(jax.random.key(seed), 7)
    return {
        "query_proj": gaussian(splits[0], (SEQUENCE_LENGTH, FEATURE_WIDTH), 1.0, 6.0, ((0, 32),)),
        "key_proj": gaussian(splits[1], (SEQUENCE_LENGTH, FEATURE_WIDTH), 1.0, 6.0, ((0, 32),)),
        "value_proj": gaussian(splits[2], (SEQUENCE_LENGTH, FEATURE_WIDTH), 1.0, 6.0, ((0, 32),)),
        "long_filter": draw_long_filter(jax.random.fold_in(splits[6], 71), 0),
        "short_filter": gaussian(splits[4], (3, 3, FEATURE_WIDTH), 0.6, 3.0, ((2, 4),), jnp.float32),
        "skip_bias": jnp.clip(0.5 + 1.0 * jax.random.uniform(splits[5], (FEATURE_WIDTH,), jnp.float32) ** block_levels(splits[5], (FEATURE_WIDTH,), ((0, 4),), -0.2, 0.2), 0.5, 1.5),
    }


def short_conv(signal, weights):
    padded = jnp.pad(signal.astype(jnp.float32), ((2, 0), (0, 0)))
    return weights[0][None, :] * padded[2:] + weights[1][None, :] * padded[1:-1] + weights[2][None, :] * padded[:-2]


def reference(query_proj, key_proj, value_proj, long_filter, short_filter, skip_bias):
    query_short = short_conv(query_proj, short_filter[0])
    key_short = short_conv(key_proj, short_filter[1])
    value_short = short_conv(value_proj, short_filter[2])
    mixed_input = key_short * value_short
    block_width = 128 if FEATURE_WIDTH % 128 == 0 else FEATURE_WIDTH
    block_count = FEATURE_WIDTH // block_width

    def transform(operands):
        signal, kernel = operands
        padded_length = 2 * SEQUENCE_LENGTH
        product = jnp.fft.rfft(signal, n=padded_length, axis=0) * jnp.fft.rfft(kernel, n=padded_length, axis=0)
        return jnp.fft.irfft(product, n=padded_length, axis=0)[:SEQUENCE_LENGTH]

    signal_blocks = mixed_input.reshape(SEQUENCE_LENGTH, block_count, block_width).transpose(1, 0, 2)
    kernel_blocks = long_filter.reshape(SEQUENCE_LENGTH, block_count, block_width).transpose(1, 0, 2)
    convolved = lax.map(transform, (signal_blocks, kernel_blocks))
    long_conv = convolved.transpose(1, 0, 2).reshape(SEQUENCE_LENGTH, FEATURE_WIDTH).astype(jnp.float32)
    return query_short * (long_conv + skip_bias[None, :] * mixed_input)
```

```python
import functools

import jax
import jax.numpy as jnp
import ml_dtypes
import numpy as np
from jax import lax
from jax.experimental import pallas as pl
from jax.experimental.pallas import tpu as pltpu
from jax.sharding import PartitionSpec as P

LANES = 128
PAD = 8
SPAN = 240.0
BOTH = ("ctx", "tp")
bf16, f32 = jnp.bfloat16, jnp.float32


def split_table(table):
    high = table.astype(ml_dtypes.bfloat16)
    low = (table - high.astype(np.float64)).astype(ml_dtypes.bfloat16)
    return np.stack([high, low])


@functools.lru_cache(maxsize=None)
def transform_tables(rows):
    m = np.arange(rows)
    k1 = np.arange(rows) + 0.5
    b = np.arange(LANES)
    outer = 2.0 * np.pi * np.outer(k1, m) / (2 * rows)
    inner = 2.0 * np.pi * (np.outer(b, b) % LANES) / LANES
    twist = 2.0 * np.pi * np.outer(k1, b) / (2 * LANES * rows)
    c, s = np.cos(inner), np.sin(inner)
    outer_forward = np.concatenate([np.cos(outer), -np.sin(outer)], 0)
    inner_forward = np.block([[c, -s], [s, c]])
    return (
        split_table(outer_forward),
        split_table(inner_forward),
        split_table(inner_forward.T),
        split_table(outer_forward.T),
        np.stack([np.cos(twist), -np.sin(twist)]).astype(np.float32),
    )


def halves(value):
    high = value.astype(bf16)
    return high, (value - high.astype(f32)).astype(bf16)


def mm(left, right):
    return jnp.dot(left, right, preferred_element_type=f32)


def product(left, right):
    return mm(left[0], right[0]) + (mm(left[1], right[0]) + mm(left[0], right[1]))


def pair(ref):
    return ref[0], ref[1]


def forward(signal, rows, outer, inner, twist):
    group = signal.shape[1] // LANES
    columns = product(pair(outer), halves(signal))
    cos, sin = twist[0], twist[1]
    stacked = []
    for p in range(group):
        re = columns[:rows, p * LANES : (p + 1) * LANES]
        im = columns[rows:, p * LANES : (p + 1) * LANES]
        stacked.append(jnp.concatenate([re * cos - im * sin, re * sin + im * cos], 1))
    return product(halves(jnp.concatenate(stacked, 0)), pair(inner))


def backward(spectrum, rows, inner, outer, twist):
    group = spectrum.shape[0] // rows
    lines = product(halves(spectrum), pair(inner))
    cos, sin = twist[0], twist[1]
    columns = []
    for p in range(group):
        re = lines[p * rows : (p + 1) * rows, :LANES]
        im = lines[p * rows : (p + 1) * rows, LANES:]
        columns.append(jnp.concatenate([re * cos + im * sin, im * cos - re * sin], 0))
    return product(pair(outer), halves(jnp.concatenate(columns, 1)))


def encode(value, inverse_scale):
    magnitude = jnp.exp2(jnp.abs(value) * inverse_scale * SPAN - SPAN / 2)
    return jnp.where(value < 0, -magnitude, magnitude)


def decode(code, scale):
    magnitude = (jnp.log2(jnp.abs(code)) + SPAN / 2) * (scale * (1.0 / SPAN))
    return jnp.where(code < 0, -magnitude, magnitude)


def block_scale(largest):
    return jnp.maximum(largest * 1.0078125, 1e-30).astype(bf16).astype(f32)


def short_conv(ext_ref, weights, length):
    return (
        weights[0:1] * ext_ref[8 : 8 + length]
        + weights[1:2] * ext_ref[7 : 7 + length]
        + weights[2:3] * ext_ref[6 : 6 + length]
    )


def fill(ext_ref, current, before):
    ext_ref[6:8] = before.astype(f32)
    ext_ref[8 : 8 + current.shape[0]] = current[...].astype(f32)


def lane_index(shape):
    return lax.broadcasted_iota(jnp.int32, shape, 1)


def rows_out_kernel(dims, idx_ref, k_ref, v_ref, halo_ref, w_ref, out_ref, k_ext, v_ext):
    length, per, parts = dims
    steps = length // LANES
    fill(k_ext, k_ref, halo_ref[2:4])
    fill(v_ext, v_ref, halo_ref[4:6])
    weights = w_ref[0]
    mixed = short_conv(k_ext, weights[3:6], length) * short_conv(v_ext, weights[6:9], length)
    codes, scales = [], []
    for step in range(steps):
        block = mixed[step * LANES : (step + 1) * LANES]
        scale = block_scale(jnp.max(jnp.abs(block), 0, keepdims=True))
        scales.append(jnp.broadcast_to(scale, (PAD, LANES)))
        codes.append(encode(block, 1.0 / scale).T)
    lane = lane_index((PAD, LANES))
    for g in range(parts):
        piece = [code[g * per : (g + 1) * per] for code in codes]
        line = jnp.ones((PAD, LANES), f32)
        for step in range(steps):
            moved = pltpu.roll(scales[step], ((step - g) * per) % LANES, 1)
            inside = (lane >= step * per) & (lane < (step + 1) * per)
            line = jnp.where(inside, moved, line)
        out_ref[g, 0] = jnp.concatenate(piece + [line], 0).astype(bf16)


def gate_parts_kernel(
    length, idx_ref, q_ref, k_ref, v_ref, halo_ref, w_ref, short_ref, skip_ref, q_ext, k_ext, v_ext
):
    fill(q_ext, q_ref, halo_ref[0:2])
    fill(k_ext, k_ref, halo_ref[2:4])
    fill(v_ext, v_ref, halo_ref[4:6])
    weights = w_ref[0]
    mixed = short_conv(k_ext, weights[3:6], length) * short_conv(v_ext, weights[6:9], length)
    short_ref[...] = short_conv(q_ext, weights[0:3], length)
    skip_ref[...] = weights[9:10] * mixed


def gate_kernel(dims, y_ref, short_ref, skip_ref, out_ref):
    length, per, parts = dims
    steps = length // LANES
    rows = steps * per
    tiles = [y_ref[g, 0].astype(f32) for g in range(parts)]
    lane = lane_index((PAD, LANES))
    for step in range(steps):
        code = jnp.concatenate([t[step * per : (step + 1) * per] for t in tiles], 0).T
        scale = jnp.ones((PAD, LANES), f32)
        for g in range(parts):
            moved = pltpu.roll(tiles[g][rows:], ((g - step) * per) % LANES, 1)
            inside = (lane >= g * per) & (lane < (g + 1) * per)
            scale = jnp.where(inside, moved, scale)
        here = pl.ds(step * LANES, LANES)
        out_ref[here, :] = short_ref[here, :] * (decode(code, scale[0:1]) + skip_ref[here, :])


def filter_rows_kernel(dims, idx_ref, h_ref, *refs):
    per, peers = dims
    outs, turned = refs[:-1], refs[-1]
    me = idx_ref[0]
    for r in range(h_ref.shape[0] // LANES):
        for c in range(h_ref.shape[1] // LANES):
            block = h_ref[r * LANES : (r + 1) * LANES, c * LANES : (c + 1) * LANES].T
            for g in range(LANES // per):
                turned[c * (LANES // per) + g] = block[g * per : (g + 1) * per]
        for s in range(peers):
            outs[s][r] = turned[lax.bitwise_xor(me, s)]


def filter_kernel(dims, idx_ref, *refs):
    rows, per, peers, group = dims
    pieces = refs[:peers]
    outer, inner, twist, out_ref, held, sems = refs[peers:]
    me = idx_ref[0]
    size = rows // peers * per
    copies = []
    for s in range(peers):
        start = pl.multiple_of(lax.bitwise_xor(me, s) * size, 8)
        copies.append(pltpu.make_async_copy(pieces[s], held.at[pl.ds(start, size)], sems.at[s]))
        copies[-1].start()
    for copy in copies:
        copy.wait()

    def body(i, carry):
        first = i * group
        signal = jnp.concatenate(
            [held[pl.ds(first + p, rows, stride=per), :] for p in range(group)], 1
        )
        spectrum = forward(signal, rows, outer, inner, twist) * (1.0 / (LANES * rows))
        for p in range(group):
            out_ref[first + p] = spectrum[p * rows : (p + 1) * rows]
        return carry

    lax.fori_loop(0, per // group, body, 0)


def conv_kernel(
    dims, x_ref, h_ref, outer, inner, inner_back, outer_back, twist, out_ref, held
):
    rows, per, lines, blocks, group = dims

    def unpack(i, carry):
        tile = x_ref[i].astype(f32)
        scale = jnp.broadcast_to(tile[lines : lines + 1], (LANES, LANES)).T[:lines]
        start = pl.multiple_of(i * lines, 8)
        held[pl.ds(start, lines), :] = decode(tile[:lines], scale)
        return carry

    lax.fori_loop(0, blocks, unpack, 0)

    def body(i, carry):
        first = i * group
        signal = jnp.concatenate(
            [held[pl.ds(first + p, rows, stride=per), :] for p in range(group)], 1
        )
        spectrum = forward(signal, rows, outer, inner, twist)
        joined = []
        for p in range(group):
            re = spectrum[p * rows : (p + 1) * rows, :LANES]
            im = spectrum[p * rows : (p + 1) * rows, LANES:]
            h_re, h_im = h_ref[first + p, :, :LANES], h_ref[first + p, :, LANES:]
            joined.append(jnp.concatenate([re * h_re - im * h_im, re * h_im + im * h_re], 1))
        result = backward(jnp.concatenate(joined, 0), rows, inner_back, outer_back, twist)
        for p in range(group):
            held[pl.ds(first + p, rows, stride=per), :] = result[:, p * LANES : (p + 1) * LANES]
        return carry

    lax.fori_loop(0, per // group, body, 0)

    def pack(i, carry):
        start = pl.multiple_of(i * lines, 8)
        tile = held[pl.ds(start, lines), :]
        scale = block_scale(jnp.max(jnp.abs(tile), 1, keepdims=True))
        code = encode(tile, 1.0 / scale)
        wide = jnp.broadcast_to(scale, (lines, LANES))
        if lines < LANES:
            wide = jnp.concatenate([wide, jnp.ones((LANES - lines, LANES), f32)], 0)
        out_ref[i] = jnp.concatenate([code, wide.T[:PAD]], 0).astype(bf16)
        return carry

    lax.fori_loop(0, blocks, pack, 0)


def whole(array):
    return pl.BlockSpec(array.shape, lambda *_: (0,) * len(array.shape))


PARAMS = dict(vmem_limit_bytes=48 * 1024 * 1024)


def local(sizes, query, key, value, long_filter, short_filter, skip_bias):
    peers, depth = sizes
    devices = peers * depth
    length, width = query.shape
    shard = long_filter.shape[1]
    per = shard // peers
    rows = length * devices // LANES
    lines = length // LANES * per
    parts = LANES // per
    tiles = shard // LANES
    group = 4
    me = jnp.stack([lax.axis_index("ctx"), lax.axis_index("tp")]).astype(jnp.int32)
    tables = transform_tables(rows)
    outer, inner, inner_back, outer_back, twist = (jnp.asarray(t) for t in tables)

    def crossed(array, axis, count):
        return [array[0]] + [
            lax.ppermute(array[s], axis, [(i, i ^ s) for i in range(count)])
            for s in range(1, count)
        ]

    edge = jnp.concatenate([query[-2:], key[-2:], value[-2:]], 0)
    halo = lax.ppermute(edge, BOTH, [(i, i + 1) for i in range(devices - 1)])
    own = jnp.concatenate([short_filter.reshape(9, shard), skip_bias[None]], 0)
    taps = jnp.stack(crossed([own] * depth, "tp", depth))

    chunk = long_filter.shape[0] // LANES
    step = min(4, chunk)
    pieces = pl.pallas_call(
        functools.partial(filter_rows_kernel, (per, peers)),
        grid_spec=pltpu.PrefetchScalarGridSpec(
            num_scalar_prefetch=1,
            grid=(chunk // step,),
            in_specs=[pl.BlockSpec((step * LANES, shard), lambda i, _: (i, 0))],
            out_specs=[pl.BlockSpec((step, per, LANES), lambda i, _: (i, 0, 0))] * peers,
            scratch_shapes=[pltpu.VMEM((peers, per, LANES), f32)],
        ),
        out_shape=[jax.ShapeDtypeStruct((chunk, per, LANES), f32)] * peers,
        compiler_params=pltpu.CompilerParams(**PARAMS),
        name="filter_rows",
    )(me, long_filter)
    pieces = crossed(pieces, "ctx", peers)
    pieces = [piece.reshape(chunk * per, LANES) for piece in pieces]

    row_spec = pl.BlockSpec((length, LANES), lambda j, _: (0, j))
    halo_spec = pl.BlockSpec((6, LANES), lambda j, _: (0, j))
    tap_spec = pl.BlockSpec(
        (1, 10, LANES), lambda j, idx: (lax.bitwise_xor(idx[1], j // tiles), 0, j % tiles)
    )
    wire_shape = jax.ShapeDtypeStruct((peers, depth, lines + PAD, LANES), bf16)
    ext = pltpu.VMEM((length + 8, LANES), f32)
    coded = pl.pallas_call(
        functools.partial(rows_out_kernel, (length, per, parts)),
        grid_spec=pltpu.PrefetchScalarGridSpec(
            num_scalar_prefetch=1,
            grid=(width // LANES,),
            in_specs=[row_spec, row_spec, halo_spec, tap_spec],
            out_specs=pl.BlockSpec(
                (parts, 1, lines + PAD, LANES), lambda j, _: (j % tiles, j // tiles, 0, 0)
            ),
            scratch_shapes=[ext] * 2,
        ),
        out_shape=wire_shape,
        compiler_params=pltpu.CompilerParams(**PARAMS),
        name="mixed_rows",
    )(me, key, value, halo, taps)
    coded = coded.reshape(devices, lines + PAD, LANES)
    arrived = lax.all_to_all(coded, BOTH, split_axis=0, concat_axis=0, tiled=True)

    spectrum = pl.pallas_call(
        functools.partial(filter_kernel, (rows, per, peers, group)),
        grid_spec=pltpu.PrefetchScalarGridSpec(
            num_scalar_prefetch=1,
            grid=(1,),
            in_specs=[pl.BlockSpec(memory_space=pl.ANY)] * peers
            + [whole(outer), whole(inner), whole(twist)],
            out_specs=pl.BlockSpec((per, rows, 2 * LANES), lambda *_: (0, 0, 0)),
            scratch_shapes=[
                pltpu.VMEM((rows * per, LANES), f32),
                pltpu.SemaphoreType.DMA((peers,)),
            ],
        ),
        out_shape=jax.ShapeDtypeStruct((per, rows, 2 * LANES), f32),
        compiler_params=pltpu.CompilerParams(**PARAMS),
        name="filter_spectrum",
    )(me, *pieces, outer, inner, twist)

    query_short, skip = pl.pallas_call(
        functools.partial(gate_parts_kernel, length),
        grid_spec=pltpu.PrefetchScalarGridSpec(
            num_scalar_prefetch=1,
            grid=(width // LANES,),
            in_specs=[row_spec, row_spec, row_spec, halo_spec, tap_spec],
            out_specs=[row_spec, row_spec],
            scratch_shapes=[ext] * 3,
        ),
        out_shape=[jax.ShapeDtypeStruct((length, width), f32)] * 2,
        compiler_params=pltpu.CompilerParams(**PARAMS),
        name="gate_parts",
    )(me, query, key, value, halo, taps)

    convolved = pl.pallas_call(
        functools.partial(conv_kernel, (rows, per, lines, devices, group)),
        out_shape=jax.ShapeDtypeStruct((devices, lines + PAD, LANES), bf16),
        scratch_shapes=[pltpu.VMEM((rows * per, LANES), f32)],
        compiler_params=pltpu.CompilerParams(**PARAMS),
        name="long_conv",
    )(arrived, spectrum, outer, inner, inner_back, outer_back, twist)
    returned = lax.all_to_all(convolved, BOTH, split_axis=0, concat_axis=0, tiled=True)
    returned = returned.reshape(peers, depth, lines + PAD, LANES)

    row_spec = pl.BlockSpec((length, LANES), lambda j: (0, j))
    return pl.pallas_call(
        functools.partial(gate_kernel, (length, per, parts)),
        grid=(width // LANES,),
        in_specs=[
            pl.BlockSpec(
                (parts, 1, lines + PAD, LANES), lambda j: (j % tiles, j // tiles, 0, 0)
            ),
            row_spec,
            row_spec,
        ],
        out_specs=row_spec,
        out_shape=jax.ShapeDtypeStruct((length, width), f32),
        compiler_params=pltpu.CompilerParams(**PARAMS),
        name="gate",
    )(returned, query_short, skip)


def solution(mesh):
    sizes = (mesh.shape["ctx"], mesh.shape["tp"])
    return jax.shard_map(
        functools.partial(local, sizes),
        mesh=mesh,
        in_specs=(
            P(BOTH, None),
            P(BOTH, None),
            P(BOTH, None),
            P("ctx", "tp"),
            P(None, None, "tp"),
            P("tp"),
        ),
        out_specs=P(BOTH, None),
        check_vma=False,
    )
```

```python
import functools

import jax
import jax.numpy as jnp
import ml_dtypes
import numpy as np
from jax import lax
from jax.experimental import pallas as pl
from jax.experimental.pallas import tpu as pltpu
from jax.sharding import PartitionSpec as P

LANES = 128
PAD = 8
SPAN = 240.0
BOTH = ("ctx", "tp")
bf16, f32 = jnp.bfloat16, jnp.float32


def split_table(table, axis):
    high = table.astype(ml_dtypes.bfloat16)
    low = (table - high.astype(np.float64)).astype(ml_dtypes.bfloat16)
    parts = [high, low, high] if axis == 1 else [high, high, low]
    return np.concatenate(parts, axis)


@functools.lru_cache(maxsize=None)
def transform_tables(rows):
    m = np.arange(rows)
    k1 = np.arange(rows) + 0.5
    b = np.arange(LANES)
    outer = 2.0 * np.pi * np.outer(k1, m) / (2 * rows)
    inner = 2.0 * np.pi * (np.outer(b, b) % LANES) / LANES
    twist = 2.0 * np.pi * np.outer(k1, b) / (2 * LANES * rows)
    c, s = np.cos(inner), np.sin(inner)
    outer_forward = np.concatenate([np.cos(outer), -np.sin(outer)], 0)
    inner_forward = np.block([[c, -s], [s, c]])
    return (
        split_table(outer_forward, 1),
        split_table(inner_forward, 0),
        split_table(inner_forward.T, 0),
        split_table(outer_forward.T, 1),
        np.stack([np.cos(twist), -np.sin(twist)]).astype(np.float32),
    )


def halves(value):
    high = value.astype(bf16)
    return high, (value - high.astype(f32)).astype(bf16)


def from_left(table, value):
    high, low = halves(value)
    return jnp.dot(table[...], jnp.concatenate([high, high, low], 0), preferred_element_type=f32)


def from_right(value, table):
    high, low = halves(value)
    return jnp.dot(jnp.concatenate([high, low, high], 1), table[...], preferred_element_type=f32)


def forward(signal, rows, outer, inner, twist):
    group = signal.shape[1] // LANES
    columns = from_left(outer, signal)
    cos, sin = twist[0], twist[1]
    stacked = []
    for p in range(group):
        re = columns[:rows, p * LANES : (p + 1) * LANES]
        im = columns[rows:, p * LANES : (p + 1) * LANES]
        stacked.append(jnp.concatenate([re * cos - im * sin, re * sin + im * cos], 1))
    return from_right(jnp.concatenate(stacked, 0), inner)


def backward(spectrum, rows, inner, outer, twist):
    group = spectrum.shape[0] // rows
    lines = from_right(spectrum, inner)
    cos, sin = twist[0], twist[1]
    columns = []
    for p in range(group):
        re = lines[p * rows : (p + 1) * rows, :LANES]
        im = lines[p * rows : (p + 1) * rows, LANES:]
        columns.append(jnp.concatenate([re * cos + im * sin, im * cos - re * sin], 0))
    return from_left(outer, jnp.concatenate(columns, 1))


def encode(value, inverse_scale):
    magnitude = jnp.exp2(jnp.abs(value) * inverse_scale * SPAN - SPAN / 2)
    return jnp.where(value < 0, -magnitude, magnitude)


def decode(code, scale):
    magnitude = (jnp.log2(jnp.abs(code)) + SPAN / 2) * (scale * (1.0 / SPAN))
    return jnp.where(code < 0, -magnitude, magnitude)


def block_scale(largest):
    return jnp.maximum(largest * 1.0078125, 1e-30).astype(bf16).astype(f32)


def short_conv(ext_ref, weights, length):
    return (
        weights[0:1] * ext_ref[8 : 8 + length]
        + weights[1:2] * ext_ref[7 : 7 + length]
        + weights[2:3] * ext_ref[6 : 6 + length]
    )


def fill(ext_ref, current, before):
    ext_ref[6:8] = before
    ext_ref[8 : 8 + current.shape[0]] = current.astype(f32)


def columns(j):
    return pl.ds(pl.multiple_of(j * LANES, LANES), LANES)


def lane_index(shape):
    return lax.broadcasted_iota(jnp.int32, shape, 1)


def edges_kernel(q_ref, k_ref, v_ref, short_ref, skip_ref, edge_ref, own_ref):
    last = q_ref.shape[0]
    shard = own_ref.shape[1]
    edge_ref[...] = jnp.zeros_like(edge_ref)
    own_ref[...] = jnp.zeros_like(own_ref)
    for i, ref in enumerate((q_ref, k_ref, v_ref)):
        edge_ref[2 * i : 2 * i + 2] = ref[...].astype(f32)[last - 2 : last]
        for ref_out in (edge_ref, own_ref):
            ref_out[6 + 3 * i : 9 + 3 * i, :shard] = short_ref[i]
    for ref_out in (edge_ref, own_ref):
        ref_out[15:16, :shard] = skip_ref[...]


def taps_and_edge(idx_ref, refs, tiles, j):
    edge_ref, *held = refs
    depth = len(held)
    behind = lax.rem(idx_ref[1] - j // tiles + depth, depth)
    here = columns(lax.rem(j, tiles))
    taps = held[0][:, here]
    for s in range(1, depth):
        taps = jnp.where(behind == s, held[s][:, here], taps)
    first = (idx_ref[0] == 0) & (idx_ref[1] == 0)
    return taps[6:15], taps[15:16], jnp.where(first, 0.0, edge_ref[0:6, columns(j)])


def column_copies(sources, targets, sems, j):
    return [
        pltpu.make_async_copy(s.at[:, columns(j)], t.at[:, columns(j)], sems.at[i, j])
        for i, (s, t) in enumerate(zip(sources, targets))
    ]


def start_all(copies_of, count):
    def step(j, carry):
        for copy in copies_of(j):
            copy.start()
        return carry

    lax.fori_loop(0, count, step, 0)


def wait_all(copies_of, count):
    def step(j, carry):
        for copy in copies_of(j):
            copy.wait()
        return carry

    lax.fori_loop(0, count, step, 0)


def rows_out_kernel(dims, idx_ref, k_hbm, v_hbm, *refs):
    length, per, parts, tiles, count = dims
    out_hbm, k_ref, v_ref, out_ref, k_ext, v_ext, sems, out_sems = refs[-8:]
    steps = length // LANES
    into = lambda j: column_copies((k_hbm, v_hbm), (k_ref, v_ref), sems, j)
    start_all(into, count)

    def out_of(j):
        where = (pl.ds(lax.rem(j, tiles) * parts, parts), pl.ds(j // tiles, 1))
        return [pltpu.make_async_copy(out_ref.at[where], out_hbm.at[where], out_sems.at[j])]

    def tile(j, carry):
        weights, _, before = taps_and_edge(idx_ref, refs[:-8], tiles, j)
        for copy in into(j):
            copy.wait()
        fill(k_ext, k_ref[:, columns(j)], before[2:4])
        fill(v_ext, v_ref[:, columns(j)], before[4:6])
        mixed = short_conv(k_ext, weights[3:6], length) * short_conv(v_ext, weights[6:9], length)
        codes, scales = [], []
        for step in range(steps):
            block = mixed[step * LANES : (step + 1) * LANES]
            scale = block_scale(jnp.max(jnp.abs(block), 0, keepdims=True))
            scales.append(jnp.broadcast_to(scale, (PAD, LANES)))
            codes.append(encode(block, 1.0 / scale).T)
        lane = lane_index((PAD, LANES))
        for g in range(parts):
            piece = [code[g * per : (g + 1) * per] for code in codes]
            line = jnp.ones((PAD, LANES), f32)
            for step in range(steps):
                moved = pltpu.roll(scales[step], ((step - g) * per) % LANES, 1)
                inside = (lane >= step * per) & (lane < (step + 1) * per)
                line = jnp.where(inside, moved, line)
            whole_piece = jnp.concatenate(piece + [line], 0).astype(bf16)
            out_ref[lax.rem(j, tiles) * parts + g, j // tiles] = whole_piece
        for copy in out_of(j):
            copy.start()
        return carry

    lax.fori_loop(0, count, tile, 0)
    wait_all(out_of, count)


def gate_parts_kernel(dims, idx_ref, q_ref, k_ref, v_ref, *refs):
    length, tiles = dims
    short_ref, skip_ref, q_ext, k_ext, v_ext = refs[-5:]
    weights, bias, before = taps_and_edge(idx_ref, refs[:-5], tiles, pl.program_id(0))
    fill(q_ext, q_ref[...], before[0:2])
    fill(k_ext, k_ref[...], before[2:4])
    fill(v_ext, v_ref[...], before[4:6])
    mixed = short_conv(k_ext, weights[3:6], length) * short_conv(v_ext, weights[6:9], length)
    short_ref[...] = short_conv(q_ext, weights[0:3], length)
    skip_ref[...] = bias * mixed


def gate_kernel(dims, y_ref, short_hbm, skip_hbm, out_hbm, short_ref, skip_ref, out_ref, sems):
    length, per, parts, tiles, count = dims
    steps = length // LANES
    rows = steps * per
    into = lambda j: column_copies((short_hbm, skip_hbm), (short_ref, skip_ref), sems, j)
    out_of = lambda j: column_copies((out_ref,), (out_hbm,), sems.at[pl.ds(2, 1)], j)
    start_all(into, count)

    def tile(j, carry):
        pieces = [
            y_ref[lax.rem(j, tiles) * parts + g, j // tiles].astype(f32) for g in range(parts)
        ]
        lane = lane_index((PAD, LANES))
        values = []
        for step in range(steps):
            code = jnp.concatenate([t[step * per : (step + 1) * per] for t in pieces], 0).T
            scale = jnp.ones((PAD, LANES), f32)
            for g in range(parts):
                moved = pltpu.roll(pieces[g][rows:], ((g - step) * per) % LANES, 1)
                inside = (lane >= g * per) & (lane < (g + 1) * per)
                scale = jnp.where(inside, moved, scale)
            values.append(decode(code, scale[0:1]))
        for copy in into(j):
            copy.wait()
        for step in range(steps):
            here = pl.ds(step * LANES, LANES)
            out_ref[here, columns(j)] = short_ref[here, columns(j)] * (
                values[step] + skip_ref[here, columns(j)]
            )
        for copy in out_of(j):
            copy.start()
        return carry

    lax.fori_loop(0, count, tile, 0)
    wait_all(out_of, count)


def filter_rows_kernel(dims, idx_ref, h_ref, *refs):
    per, peers, chunk = dims
    outs, turned, lines = refs[:peers], refs[-2], refs[-1]
    me = idx_ref[0]
    parts = LANES // per
    for r in range(chunk):
        for c in range(h_ref.shape[1] // LANES):
            block = h_ref[r * LANES : (r + 1) * LANES, c * LANES : (c + 1) * LANES]
            scale = block_scale(jnp.max(jnp.abs(block), 0, keepdims=True))
            code = encode(block, 1.0 / scale).T.astype(bf16)
            wide = jnp.broadcast_to(scale, (PAD, LANES))
            for g in range(parts):
                turned[c * parts + g, r] = code[g * per : (g + 1) * per]
                lines[c * parts + g, r : r + 1] = pltpu.roll(wide, (-g * per) % LANES, 1)[0:1]
    for s in range(peers):
        peer = lax.bitwise_xor(me, s)
        outs[s][0 : chunk * per] = turned[peer].reshape(chunk * per, LANES)
        outs[s][chunk * per :] = lines[peer].astype(bf16)


def filter_kernel(dims, idx_ref, *refs):
    rows, per, peers, group = dims
    pieces = refs[:peers]
    outer, inner, twist, out_hbm, out_ref, coded, scales, held, wide, sems, out_sems = refs[peers:]
    me = idx_ref[0]
    chunk = rows // peers
    size = chunk * per
    copies = []
    for s in range(peers):
        peer = lax.bitwise_xor(me, s)
        copies.append(
            pltpu.make_async_copy(
                pieces[s].at[pl.ds(0, size)],
                coded.at[pl.ds(pl.multiple_of(peer * size, 16), size)],
                sems.at[0, s],
            )
        )
        copies.append(
            pltpu.make_async_copy(
                pieces[s].at[pl.ds(size, chunk)],
                scales.at[pl.ds(pl.multiple_of(peer * chunk, 16), chunk)],
                sems.at[1, s],
            )
        )
    for copy in copies:
        copy.start()
    for copy in copies:
        copy.wait()
    wide[...] = scales[...].astype(f32)

    def out_of(i):
        where = pl.ds(i * group, group)
        return [pltpu.make_async_copy(out_ref.at[where], out_hbm.at[where], out_sems.at[i])]

    def widen(i, carry):
        here = pl.ds(pl.multiple_of(i * size, 16), size)
        held[here, :] = coded[here, :].astype(f32)
        return carry

    lax.fori_loop(0, peers, widen, 0)

    def body(i, carry):
        first = i * group
        near = pltpu.roll(wide[...], LANES - first, 1)
        signal = jnp.concatenate(
            [
                decode(held[pl.ds(first + p, rows, stride=per), :], near[:, p : p + 1])
                for p in range(group)
            ],
            1,
        )
        spectrum = forward(signal, rows, outer, inner, twist) * (1.0 / (LANES * rows))
        for p in range(group):
            out_ref[first + p] = spectrum[p * rows : (p + 1) * rows]
        for copy in out_of(i):
            copy.start()
        return carry

    lax.fori_loop(0, per // group, body, 0)
    wait_all(out_of, per // group)


def conv_kernel(
    dims, x_ref, h_hbm, outer, inner, inner_back, outer_back, twist, out_ref, held, h_ref, sem
):
    rows, per, lines, blocks, group, batch = dims
    fetch = pltpu.make_async_copy(h_hbm, h_ref, sem)
    fetch.start()

    def unpack(i, carry):
        for j in range(batch):
            tile = x_ref[i * batch + j].astype(f32)
            scale = jnp.broadcast_to(tile[lines : lines + 1], (LANES, LANES)).T[:lines]
            start = pl.multiple_of((i * batch + j) * lines, 8)
            held[pl.ds(start, lines), :] = decode(tile[:lines], scale)
        return carry

    lax.fori_loop(0, blocks // batch, unpack, 0)
    fetch.wait()

    def body(i, carry):
        first = i * group
        signal = jnp.concatenate(
            [held[pl.ds(first + p, rows, stride=per), :] for p in range(group)], 1
        )
        spectrum = forward(signal, rows, outer, inner, twist)
        joined = []
        for p in range(group):
            re = spectrum[p * rows : (p + 1) * rows, :LANES]
            im = spectrum[p * rows : (p + 1) * rows, LANES:]
            h_re, h_im = h_ref[first + p, :, :LANES], h_ref[first + p, :, LANES:]
            joined.append(jnp.concatenate([re * h_re - im * h_im, re * h_im + im * h_re], 1))
        result = backward(jnp.concatenate(joined, 0), rows, inner_back, outer_back, twist)
        for p in range(group):
            held[pl.ds(first + p, rows, stride=per), :] = result[:, p * LANES : (p + 1) * LANES]
        return carry

    lax.fori_loop(0, per // group, body, 0)

    def pack(i, carry):
        for j in range(batch):
            start = pl.multiple_of((i * batch + j) * lines, 8)
            tile = held[pl.ds(start, lines), :]
            scale = block_scale(jnp.max(jnp.abs(tile), 1, keepdims=True))
            code = encode(tile, 1.0 / scale)
            wide = jnp.broadcast_to(scale, (lines, LANES))
            if lines < LANES:
                wide = jnp.concatenate([wide, jnp.ones((LANES - lines, LANES), f32)], 0)
            out_ref[i * batch + j] = jnp.concatenate([code, wide.T[:PAD]], 0).astype(bf16)
        return carry

    lax.fori_loop(0, blocks // batch, pack, 0)


def whole(array):
    return pl.BlockSpec(array.shape, lambda *_: (0,) * len(array.shape))


def vmem_limit(mebibytes):
    return pltpu.CompilerParams(vmem_limit_bytes=mebibytes * 1024 * 1024)


def local(sizes, query, key, value, long_filter, short_filter, skip_bias):
    peers, depth = sizes
    devices = peers * depth
    length, width = query.shape
    shard = long_filter.shape[1]
    per = shard // peers
    rows = length * devices // LANES
    lines = length // LANES * per
    parts = LANES // per
    tiles = shard // LANES
    group = min(8, per)
    me = jnp.stack([lax.axis_index(axis) for axis in BOTH]).astype(jnp.int32)
    tables = transform_tables(rows)
    outer, inner, inner_back, outer_back, twist = (jnp.asarray(t) for t in tables)

    def crossed(array, axis, count):
        return [array[0]] + [
            lax.ppermute(array[s], axis, [(i, i ^ s) for i in range(count)])
            for s in range(1, count)
        ]

    query, key, value = (pltpu.with_memory_space_constraint(a, pltpu.HBM) for a in (query, key, value))
    last = pl.BlockSpec((16, width), lambda i: (length // 16 - 1, 0))
    edge, own = pl.pallas_call(
        edges_kernel,
        grid=(1,),
        in_specs=[last] * 3 + [whole(short_filter), pl.BlockSpec((1, shard), lambda i: (0, 0))],
        out_specs=[
            pl.BlockSpec((16, width), lambda i: (0, 0)),
            pl.BlockSpec((16, shard), lambda i: (0, 0)),
        ],
        out_shape=[
            jax.ShapeDtypeStruct((16, width), f32),
            jax.ShapeDtypeStruct((16, shard), f32),
        ],
        compiler_params=vmem_limit(8),
        name="edges",
    )(query, key, value, short_filter, skip_bias.reshape(1, shard))

    def shifted(array, by):
        return lax.ppermute(array, BOTH, [(i, (i + by) % devices) for i in range(devices)])

    edge = shifted(edge, 1)
    taps = [own, edge] + [shifted(own, s) for s in range(2, depth)]

    chunk = long_filter.shape[0] // LANES
    pieces = pl.pallas_call(
        functools.partial(filter_rows_kernel, (per, peers, chunk)),
        grid_spec=pltpu.PrefetchScalarGridSpec(
            num_scalar_prefetch=1,
            grid=(1,),
            in_specs=[whole(long_filter)],
            out_specs=[pl.BlockSpec((chunk * per + chunk, LANES), lambda *_: (0, 0))] * peers,
            scratch_shapes=[
                pltpu.VMEM((peers, chunk, per, LANES), bf16),
                pltpu.VMEM((peers, chunk, LANES), f32),
            ],
        ),
        out_shape=[jax.ShapeDtypeStruct((chunk * per + chunk, LANES), bf16)] * peers,
        compiler_params=vmem_limit(16),
        name="filter_rows",
    )(me, long_filter)
    edge, *taps = lax.optimization_barrier((edge, *taps, *pieces))
    taps, pieces = taps[:depth], taps[depth:]
    pieces = crossed(pieces, "ctx", peers)

    row_spec = pl.BlockSpec((length, LANES), lambda j, _: (0, j))
    wire_shape = jax.ShapeDtypeStruct((peers, depth, lines + PAD, LANES), bf16)
    ext = pltpu.VMEM((length + 8, LANES), f32)
    vmem, hbm = pl.BlockSpec(memory_space=pltpu.VMEM), pl.BlockSpec(memory_space=pltpu.HBM)
    count = width // LANES
    coded = pl.pallas_call(
        functools.partial(rows_out_kernel, (length, per, parts, tiles, count)),
        in_specs=[pl.BlockSpec(memory_space=pltpu.SMEM), hbm, hbm] + [vmem] * (depth + 1),
        out_specs=hbm,
        out_shape=wire_shape,
        scratch_shapes=[
            pltpu.VMEM((length, width), bf16),
            pltpu.VMEM((length, width), bf16),
            pltpu.VMEM(wire_shape.shape, bf16),
            ext,
            ext,
            pltpu.SemaphoreType.DMA((2, count)),
            pltpu.SemaphoreType.DMA((count,)),
        ],
        compiler_params=vmem_limit(16),
        name="mixed_rows",
    )(me, key, value, edge, *taps)
    coded = coded.reshape(devices, lines + PAD, LANES)
    arrived = lax.all_to_all(coded, BOTH, split_axis=0, concat_axis=0, tiled=True)

    spectrum = pl.pallas_call(
        functools.partial(filter_kernel, (rows, per, peers, group)),
        grid_spec=pltpu.PrefetchScalarGridSpec(
            num_scalar_prefetch=1,
            grid=(1,),
            in_specs=[pl.BlockSpec(memory_space=pltpu.HBM)] * peers
            + [whole(outer), whole(inner), whole(twist)],
            out_specs=hbm,
            scratch_shapes=[
                pltpu.VMEM((per, rows, 2 * LANES), f32),
                pltpu.VMEM((rows * per, LANES), bf16),
                pltpu.VMEM((rows, LANES), bf16),
                pltpu.VMEM((rows * per, LANES), f32),
                pltpu.VMEM((rows, LANES), f32),
                pltpu.SemaphoreType.DMA((2, peers)),
                pltpu.SemaphoreType.DMA((per // group,)),
            ],
        ),
        out_shape=pltpu.HBM((per, rows, 2 * LANES), f32),
        compiler_params=vmem_limit(28),
        name="filter_spectrum",
    )(me, *pieces, outer, inner, twist)

    query_short, skip = pl.pallas_call(
        functools.partial(gate_parts_kernel, (length, tiles)),
        grid_spec=pltpu.PrefetchScalarGridSpec(
            num_scalar_prefetch=1,
            grid=(width // LANES,),
            in_specs=[row_spec] * 3 + [whole(edge)] + [whole(tap) for tap in taps],
            out_specs=[row_spec, row_spec],
            scratch_shapes=[ext] * 3,
        ),
        out_shape=[pltpu.HBM((length, width), f32)] * 2,
        compiler_params=vmem_limit(12),
        name="gate_parts",
    )(me, query, key, value, edge, *taps)

    query_short, skip, spectrum = (
        pltpu.with_memory_space_constraint(a, pltpu.HBM) for a in (query_short, skip, spectrum)
    )

    convolved = pl.pallas_call(
        functools.partial(conv_kernel, (rows, per, lines, devices, group, 4)),
        in_specs=[vmem, hbm] + [vmem] * 5,
        out_specs=vmem,
        out_shape=jax.ShapeDtypeStruct((devices, lines + PAD, LANES), bf16),
        scratch_shapes=[
            pltpu.VMEM((rows * per, LANES), f32),
            pltpu.VMEM((per, rows, 2 * LANES), f32),
            pltpu.SemaphoreType.DMA,
        ],
        compiler_params=vmem_limit(28),
        name="long_conv",
    )(arrived, spectrum, outer, inner, inner_back, outer_back, twist)
    returned = lax.all_to_all(convolved, BOTH, split_axis=0, concat_axis=0, tiled=True)
    returned = returned.reshape(peers, depth, lines + PAD, LANES)

    return pl.pallas_call(
        functools.partial(gate_kernel, (length, per, parts, tiles, count)),
        in_specs=[vmem, hbm, hbm],
        out_specs=hbm,
        out_shape=jax.ShapeDtypeStruct((length, width), f32),
        scratch_shapes=[pltpu.VMEM((length, width), f32)] * 3
        + [pltpu.SemaphoreType.DMA((3, count))],
        compiler_params=vmem_limit(20),
        name="gate",
    )(returned, query_short, skip)


def solution(mesh):
    sizes = (mesh.shape["ctx"], mesh.shape["tp"])
    return jax.shard_map(
        functools.partial(local, sizes),
        mesh=mesh,
        in_specs=(
            P(BOTH, None),
            P(BOTH, None),
            P(BOTH, None),
            P("ctx", "tp"),
            P(None, None, "tp"),
            P("tp"),
        ),
        out_specs=P(BOTH, None),
        check_vma=False,
    )
```

```python
import functools

import jax
import jax.numpy as jnp
import ml_dtypes
import numpy as np
from jax import lax
from jax.experimental import pallas as pl
from jax.experimental.pallas import tpu as pltpu
from jax.sharding import PartitionSpec as P

LANES = 128
PAD = 8
SPAN = 240.0
BOTH = ("ctx", "tp")
bf16, f32 = jnp.bfloat16, jnp.float32


def split_table(table, axis):
    high = table.astype(ml_dtypes.bfloat16)
    low = (table - high.astype(np.float64)).astype(ml_dtypes.bfloat16)
    parts = [high, low, high] if axis == 1 else [high, high, low]
    return np.concatenate(parts, axis)


@functools.lru_cache(maxsize=None)
def transform_tables(rows):
    m = np.arange(rows)
    k1 = np.arange(rows) + 0.5
    b = np.arange(LANES)
    outer = 2.0 * np.pi * np.outer(k1, m) / (2 * rows)
    inner = 2.0 * np.pi * (np.outer(b, b) % LANES) / LANES
    twist = 2.0 * np.pi * np.outer(k1, b) / (2 * LANES * rows)
    c, s = np.cos(inner), np.sin(inner)
    outer_forward = np.concatenate([np.cos(outer), -np.sin(outer)], 0)
    inner_forward = np.block([[c, -s], [s, c]])
    return (
        split_table(outer_forward, 1),
        split_table(inner_forward, 0),
        split_table(inner_forward.T, 0),
        split_table(outer_forward.T, 1),
        np.stack([np.cos(twist), -np.sin(twist)]).astype(np.float32),
    )


def halves(value):
    high = value.astype(bf16)
    return high, (value - high.astype(f32)).astype(bf16)


def from_left(table, value):
    high, low = halves(value)
    return jnp.dot(table[...], jnp.concatenate([high, high, low], 0), preferred_element_type=f32)


def from_right(value, table):
    high, low = halves(value)
    return jnp.dot(jnp.concatenate([high, low, high], 1), table[...], preferred_element_type=f32)


def forward(signal, rows, outer, inner, twist):
    group = signal.shape[1] // LANES
    columns = from_left(outer, signal)
    cos, sin = twist[0], twist[1]
    stacked = []
    for p in range(group):
        re = columns[:rows, p * LANES : (p + 1) * LANES]
        im = columns[rows:, p * LANES : (p + 1) * LANES]
        stacked.append(jnp.concatenate([re * cos - im * sin, re * sin + im * cos], 1))
    return from_right(jnp.concatenate(stacked, 0), inner)


def backward(spectrum, rows, inner, outer, twist):
    group = spectrum.shape[0] // rows
    lines = from_right(spectrum, inner)
    cos, sin = twist[0], twist[1]
    columns = []
    for p in range(group):
        re = lines[p * rows : (p + 1) * rows, :LANES]
        im = lines[p * rows : (p + 1) * rows, LANES:]
        columns.append(jnp.concatenate([re * cos + im * sin, im * cos - re * sin], 0))
    return from_left(outer, jnp.concatenate(columns, 1))


def encode(value, inverse_scale):
    magnitude = jnp.exp2(jnp.abs(value) * inverse_scale * SPAN - SPAN / 2)
    return jnp.where(value < 0, -magnitude, magnitude)


def decode(code, scale):
    magnitude = (jnp.log2(jnp.abs(code)) + SPAN / 2) * (scale * (1.0 / SPAN))
    return jnp.where(code < 0, -magnitude, magnitude)


def block_scale(largest):
    return jnp.maximum(largest * 1.0078125, 1e-30).astype(bf16).astype(f32)


def short_conv(ext_ref, weights, length):
    return (
        weights[0:1] * ext_ref[8 : 8 + length]
        + weights[1:2] * ext_ref[7 : 7 + length]
        + weights[2:3] * ext_ref[6 : 6 + length]
    )


def fill(ext_ref, current, before):
    ext_ref[6:8] = before
    ext_ref[8 : 8 + current.shape[0]] = current.astype(f32)


def columns(j):
    return pl.ds(pl.multiple_of(j * LANES, LANES), LANES)


def lane_index(shape):
    return lax.broadcasted_iota(jnp.int32, shape, 1)


def edges_kernel(q_ref, k_ref, v_ref, short_ref, skip_ref, edge_ref, own_ref, rows_ref):
    last = q_ref.shape[0]
    shard = own_ref.shape[1]
    rows_ref[...] = jnp.zeros_like(rows_ref)
    own_ref[0:6] = jnp.zeros((6, shard), f32)
    for i, ref in enumerate((q_ref, k_ref, v_ref)):
        rows_ref[2 * i : 2 * i + 2] = ref[...].astype(f32)[last - 2 : last]
        own_ref[6 + 3 * i : 9 + 3 * i] = short_ref[i]
    own_ref[15:16] = skip_ref[...]
    rest = own_ref[6:16]
    for i in range(3):
        part = rest.astype(bf16).astype(f32)
        rows_ref[6:16, i * shard : (i + 1) * shard] = part
        rest = rest - part
    edge_ref[...] = rows_ref[...].astype(bf16)


def taps_and_edge(idx_ref, refs, tiles, j):
    edge_ref, *held = refs
    depth = len(held) + 1
    behind = lax.rem(idx_ref[1] - j // tiles + depth, depth)
    tile = lax.rem(j, tiles)
    parts = [edge_ref[:, columns(tile + i * tiles)].astype(f32) for i in range(3)]
    taps = jnp.where(behind == 1, parts[0] + parts[1] + parts[2], held[0][:, columns(tile)])
    for s in range(2, depth):
        taps = jnp.where(behind == s, held[s - 1][:, columns(tile)], taps)
    first = (idx_ref[0] == 0) & (idx_ref[1] == 0)
    before = edge_ref[:, columns(j)].astype(f32)[0:6]
    return taps[6:15], taps[15:16], jnp.where(first, 0.0, before)


def column_copies(sources, targets, sems, j):
    return [
        pltpu.make_async_copy(s.at[:, columns(j)], t.at[:, columns(j)], sems.at[i, j])
        for i, (s, t) in enumerate(zip(sources, targets))
    ]


def start_all(copies_of, count):
    def step(j, carry):
        for copy in copies_of(j):
            copy.start()
        return carry

    lax.fori_loop(0, count, step, 0)


def wait_all(copies_of, count):
    def step(j, carry):
        for copy in copies_of(j):
            copy.wait()
        return carry

    lax.fori_loop(0, count, step, 0)


def rows_out_kernel(dims, idx_ref, k_hbm, v_hbm, *refs):
    length, per, parts, tiles, count = dims
    out_hbm, k_ref, v_ref, out_ref, k_ext, v_ext, sems, out_sems = refs[-8:]
    steps = length // LANES
    into = lambda j: column_copies((k_hbm, v_hbm), (k_ref, v_ref), sems, j)
    start_all(into, count)

    def out_of(j):
        where = (pl.ds(lax.rem(j, tiles) * parts, parts), pl.ds(j // tiles, 1))
        return [pltpu.make_async_copy(out_ref.at[where], out_hbm.at[where], out_sems.at[j])]

    def tile(j, carry):
        weights, _, before = taps_and_edge(idx_ref, refs[:-8], tiles, j)
        for copy in into(j):
            copy.wait()
        fill(k_ext, k_ref[:, columns(j)], before[2:4])
        fill(v_ext, v_ref[:, columns(j)], before[4:6])
        mixed = short_conv(k_ext, weights[3:6], length) * short_conv(v_ext, weights[6:9], length)
        codes, scales = [], []
        for step in range(steps):
            block = mixed[step * LANES : (step + 1) * LANES]
            scale = block_scale(jnp.max(jnp.abs(block), 0, keepdims=True))
            scales.append(jnp.broadcast_to(scale, (PAD, LANES)))
            codes.append(encode(block, 1.0 / scale).astype(bf16).T.astype(f32))
        lane = lane_index((PAD, LANES))
        for g in range(parts):
            piece = [code[g * per : (g + 1) * per] for code in codes]
            line = jnp.ones((PAD, LANES), f32)
            for step in range(steps):
                moved = pltpu.roll(scales[step], ((step - g) * per) % LANES, 1)
                inside = (lane >= step * per) & (lane < (step + 1) * per)
                line = jnp.where(inside, moved, line)
            whole_piece = jnp.concatenate(piece + [line], 0).astype(bf16)
            out_ref[lax.rem(j, tiles) * parts + g, j // tiles] = whole_piece
        for copy in out_of(j):
            copy.start()
        return carry

    lax.fori_loop(0, count, tile, 0)
    wait_all(out_of, count)


def gate_parts_kernel(dims, idx_ref, q_ref, k_ref, v_ref, *refs):
    length, tiles = dims
    short_ref, skip_ref, q_ext, k_ext, v_ext = refs[-5:]
    weights, bias, before = taps_and_edge(idx_ref, refs[:-5], tiles, pl.program_id(0))
    fill(q_ext, q_ref[...], before[0:2])
    fill(k_ext, k_ref[...], before[2:4])
    fill(v_ext, v_ref[...], before[4:6])
    mixed = short_conv(k_ext, weights[3:6], length) * short_conv(v_ext, weights[6:9], length)
    short_ref[...] = short_conv(q_ext, weights[0:3], length)
    skip_ref[...] = bias * mixed


def gate_kernel(dims, y_ref, short_hbm, skip_hbm, out_hbm, short_ref, skip_ref, out_ref, sems):
    length, per, parts, tiles, count = dims
    steps = length // LANES
    rows = steps * per
    into = lambda j: column_copies((short_hbm, skip_hbm), (short_ref, skip_ref), sems, j)
    out_of = lambda j: column_copies((out_ref,), (out_hbm,), sems.at[pl.ds(2, 1)], j)
    start_all(into, count)

    def tile(j, carry):
        pieces = [
            y_ref[lax.rem(j, tiles) * parts + g, j // tiles].astype(f32) for g in range(parts)
        ]
        lane = lane_index((PAD, LANES))
        values = []
        for step in range(steps):
            code = jnp.concatenate([t[step * per : (step + 1) * per] for t in pieces], 0).T
            scale = jnp.ones((PAD, LANES), f32)
            for g in range(parts):
                moved = pltpu.roll(pieces[g][rows:], ((g - step) * per) % LANES, 1)
                inside = (lane >= g * per) & (lane < (g + 1) * per)
                scale = jnp.where(inside, moved, scale)
            values.append(decode(code, scale[0:1]))
        for copy in into(j):
            copy.wait()
        for step in range(steps):
            here = pl.ds(step * LANES, LANES)
            out_ref[here, columns(j)] = short_ref[here, columns(j)] * (
                values[step] + skip_ref[here, columns(j)]
            )
        for copy in out_of(j):
            copy.start()
        return carry

    lax.fori_loop(0, count, tile, 0)
    wait_all(out_of, count)


def filter_rows_kernel(dims, idx_ref, h_ref, *refs):
    per, peers, chunk = dims
    outs, turned, lines = refs[:peers], refs[-2], refs[-1]
    me = idx_ref[0]
    parts = LANES // per
    for r in range(chunk):
        for c in range(h_ref.shape[1] // LANES):
            block = h_ref[r * LANES : (r + 1) * LANES, c * LANES : (c + 1) * LANES]
            scale = block_scale(jnp.max(jnp.abs(block), 0, keepdims=True))
            code = encode(block, 1.0 / scale).T.astype(bf16)
            wide = jnp.broadcast_to(scale, (PAD, LANES))
            for g in range(parts):
                turned[c * parts + g, r] = code[g * per : (g + 1) * per]
                lines[c * parts + g, r : r + 1] = pltpu.roll(wide, (-g * per) % LANES, 1)[0:1]
    for s in range(peers):
        peer = lax.bitwise_xor(me, s)
        outs[s][0 : chunk * per] = turned[peer].reshape(chunk * per, LANES)
        outs[s][chunk * per :] = lines[peer].astype(bf16)


def filter_kernel(dims, idx_ref, *refs):
    rows, per, peers, group = dims
    pieces = refs[:peers]
    outer, inner, twist, out_hbm, out_ref, coded, scales, held, wide, sems, out_sems = refs[peers:]
    me = idx_ref[0]
    chunk = rows // peers
    size = chunk * per
    copies = []
    for s in range(peers):
        peer = lax.bitwise_xor(me, s)
        copies.append(
            pltpu.make_async_copy(
                pieces[s].at[pl.ds(0, size)],
                coded.at[pl.ds(pl.multiple_of(peer * size, 16), size)],
                sems.at[0, s],
            )
        )
        copies.append(
            pltpu.make_async_copy(
                pieces[s].at[pl.ds(size, chunk)],
                scales.at[pl.ds(pl.multiple_of(peer * chunk, 16), chunk)],
                sems.at[1, s],
            )
        )
    for copy in copies:
        copy.start()
    for copy in copies:
        copy.wait()
    wide[...] = scales[...].astype(f32)

    def out_of(i):
        where = pl.ds(i * group, group)
        return [pltpu.make_async_copy(out_ref.at[where], out_hbm.at[where], out_sems.at[i])]

    def widen(i, carry):
        here = pl.ds(pl.multiple_of(i * size, 16), size)
        held[here, :] = coded[here, :].astype(f32)
        return carry

    lax.fori_loop(0, peers, widen, 0)

    def body(i, carry):
        first = i * group
        near = pltpu.roll(wide[...], LANES - first, 1)
        signal = jnp.concatenate(
            [
                decode(held[pl.ds(first + p, rows, stride=per), :], near[:, p : p + 1])
                for p in range(group)
            ],
            1,
        )
        spectrum = forward(signal, rows, outer, inner, twist) * (1.0 / (LANES * rows))
        for p in range(group):
            out_ref[first + p] = spectrum[p * rows : (p + 1) * rows]
        for copy in out_of(i):
            copy.start()
        return carry

    lax.fori_loop(0, per // group, body, 0)
    wait_all(out_of, per // group)


def conv_kernel(
    dims, x_ref, h_hbm, outer, inner, inner_back, outer_back, twist, out_ref, held, h_ref, sem
):
    rows, per, lines, blocks, group, batch = dims
    fetch = pltpu.make_async_copy(h_hbm, h_ref, sem)
    fetch.start()

    def unpack(i, carry):
        for j in range(batch):
            tile = x_ref[i * batch + j].astype(f32)
            scale = jnp.broadcast_to(tile[lines : lines + 1], (LANES, LANES)).T[:lines]
            start = pl.multiple_of((i * batch + j) * lines, 8)
            held[pl.ds(start, lines), :] = decode(tile[:lines], scale)
        return carry

    lax.fori_loop(0, blocks // batch, unpack, 0)
    fetch.wait()

    def body(i, carry):
        first = i * group
        signal = jnp.concatenate(
            [held[pl.ds(first + p, rows, stride=per), :] for p in range(group)], 1
        )
        spectrum = forward(signal, rows, outer, inner, twist)
        joined = []
        for p in range(group):
            re = spectrum[p * rows : (p + 1) * rows, :LANES]
            im = spectrum[p * rows : (p + 1) * rows, LANES:]
            h_re, h_im = h_ref[first + p, :, :LANES], h_ref[first + p, :, LANES:]
            joined.append(jnp.concatenate([re * h_re - im * h_im, re * h_im + im * h_re], 1))
        result = backward(jnp.concatenate(joined, 0), rows, inner_back, outer_back, twist)
        for p in range(group):
            held[pl.ds(first + p, rows, stride=per), :] = result[:, p * LANES : (p + 1) * LANES]
        return carry

    lax.fori_loop(0, per // group, body, 0)

    def pack(i, carry):
        for j in range(batch):
            start = pl.multiple_of((i * batch + j) * lines, 8)
            tile = held[pl.ds(start, lines), :]
            scale = block_scale(jnp.max(jnp.abs(tile), 1, keepdims=True))
            code = encode(tile, 1.0 / scale)
            wide = jnp.broadcast_to(scale, (lines, LANES))
            if lines < LANES:
                wide = jnp.concatenate([wide, jnp.ones((LANES - lines, LANES), f32)], 0)
            out_ref[i * batch + j] = jnp.concatenate([code, wide.T[:PAD]], 0).astype(bf16)
        return carry

    lax.fori_loop(0, blocks // batch, pack, 0)


def whole(array):
    return pl.BlockSpec(array.shape, lambda *_: (0,) * len(array.shape))


def vmem_limit(mebibytes):
    return pltpu.CompilerParams(vmem_limit_bytes=mebibytes * 1024 * 1024)


def local(sizes, query, key, value, long_filter, short_filter, skip_bias):
    peers, depth = sizes
    devices = peers * depth
    length, width = query.shape
    shard = long_filter.shape[1]
    per = shard // peers
    rows = length * devices // LANES
    lines = length // LANES * per
    parts = LANES // per
    tiles = shard // LANES
    group = min(8, per)
    me = jnp.stack([lax.axis_index(axis) for axis in BOTH]).astype(jnp.int32)
    tables = transform_tables(rows)
    outer, inner, inner_back, outer_back, twist = (jnp.asarray(t) for t in tables)

    def crossed(array, axis, count):
        return [array[0]] + [
            lax.ppermute(array[s], axis, [(i, i ^ s) for i in range(count)])
            for s in range(1, count)
        ]

    query, key, value = (pltpu.with_memory_space_constraint(a, pltpu.HBM) for a in (query, key, value))
    last = pl.BlockSpec((16, width), lambda i: (length // 16 - 1, 0))
    taps_hbm, bias_hbm = (
        pltpu.with_memory_space_constraint(a, pltpu.HBM)
        for a in (short_filter, skip_bias.reshape(1, shard))
    )
    edge, own = pl.pallas_call(
        edges_kernel,
        grid=(1,),
        in_specs=[last] * 3 + [whole(short_filter), pl.BlockSpec((1, shard), lambda i: (0, 0))],
        out_specs=[
            pl.BlockSpec((16, width), lambda i: (0, 0)),
            pl.BlockSpec((16, shard), lambda i: (0, 0)),
        ],
        out_shape=[
            jax.ShapeDtypeStruct((16, width), bf16),
            jax.ShapeDtypeStruct((16, shard), f32),
        ],
        scratch_shapes=[pltpu.VMEM((16, width), f32)],
        compiler_params=vmem_limit(8),
        name="edges",
    )(query, key, value, taps_hbm, bias_hbm)

    def shifted(array, by):
        return lax.ppermute(array, BOTH, [(i, (i + by) % devices) for i in range(devices)])

    edge = shifted(edge, 1)
    taps = [own] + [shifted(own, s) for s in range(2, depth)]

    chunk = long_filter.shape[0] // LANES
    pieces = pl.pallas_call(
        functools.partial(filter_rows_kernel, (per, peers, chunk)),
        grid_spec=pltpu.PrefetchScalarGridSpec(
            num_scalar_prefetch=1,
            grid=(1,),
            in_specs=[whole(long_filter)],
            out_specs=[pl.BlockSpec((chunk * per + chunk, LANES), lambda *_: (0, 0))] * peers,
            scratch_shapes=[
                pltpu.VMEM((peers, chunk, per, LANES), bf16),
                pltpu.VMEM((peers, chunk, LANES), f32),
            ],
        ),
        out_shape=[pltpu.HBM((chunk * per + chunk, LANES), bf16)] * peers,
        compiler_params=vmem_limit(16),
        name="filter_rows",
    )(me, long_filter)
    pieces = list(pieces)
    early = [s for s in (2, 4) if s < peers]
    edge, *ready = lax.optimization_barrier((edge, *taps[1:], *(pieces[s] for s in early)))
    taps[1:] = ready[: depth - 2]
    for s, piece in zip(early, ready[depth - 2 :]):
        pieces[s] = piece
    pieces = crossed(pieces, "ctx", peers)

    row_spec = pl.BlockSpec((length, LANES), lambda j, _: (0, j))
    wire_shape = jax.ShapeDtypeStruct((peers, depth, lines + PAD, LANES), bf16)
    ext = pltpu.VMEM((length + 8, LANES), f32)
    vmem, hbm = pl.BlockSpec(memory_space=pltpu.VMEM), pl.BlockSpec(memory_space=pltpu.HBM)
    count = width // LANES
    coded = pl.pallas_call(
        functools.partial(rows_out_kernel, (length, per, parts, tiles, count)),
        in_specs=[pl.BlockSpec(memory_space=pltpu.SMEM), hbm, hbm] + [vmem] * depth,
        out_specs=hbm,
        out_shape=wire_shape,
        scratch_shapes=[
            pltpu.VMEM((length, width), bf16),
            pltpu.VMEM((length, width), bf16),
            pltpu.VMEM(wire_shape.shape, bf16),
            ext,
            ext,
            pltpu.SemaphoreType.DMA((2, count)),
            pltpu.SemaphoreType.DMA((count,)),
        ],
        compiler_params=vmem_limit(16),
        name="mixed_rows",
    )(me, key, value, edge, *taps)
    coded, *ready = lax.optimization_barrier((coded, *(pieces[s] for s in early)))
    for s, piece in zip(early, ready):
        pieces[s] = piece
    coded = coded.reshape(devices, lines + PAD, LANES)
    arrived = lax.all_to_all(coded, BOTH, split_axis=0, concat_axis=0, tiled=True)

    spectrum = pl.pallas_call(
        functools.partial(filter_kernel, (rows, per, peers, group)),
        grid_spec=pltpu.PrefetchScalarGridSpec(
            num_scalar_prefetch=1,
            grid=(1,),
            in_specs=[pl.BlockSpec(memory_space=pltpu.HBM)] * peers
            + [whole(outer), whole(inner), whole(twist)],
            out_specs=hbm,
            scratch_shapes=[
                pltpu.VMEM((per, rows, 2 * LANES), f32),
                pltpu.VMEM((rows * per, LANES), bf16),
                pltpu.VMEM((rows, LANES), bf16),
                pltpu.VMEM((rows * per, LANES), f32),
                pltpu.VMEM((rows, LANES), f32),
                pltpu.SemaphoreType.DMA((2, peers)),
                pltpu.SemaphoreType.DMA((per // group,)),
            ],
        ),
        out_shape=pltpu.HBM((per, rows, 2 * LANES), f32),
        compiler_params=vmem_limit(28),
        name="filter_spectrum",
    )(me, *pieces, outer, inner, twist)

    query_short, skip = pl.pallas_call(
        functools.partial(gate_parts_kernel, (length, tiles)),
        grid_spec=pltpu.PrefetchScalarGridSpec(
            num_scalar_prefetch=1,
            grid=(width // LANES,),
            in_specs=[row_spec] * 3 + [whole(edge)] + [whole(tap) for tap in taps],
            out_specs=[row_spec, row_spec],
            scratch_shapes=[ext] * 3,
        ),
        out_shape=[pltpu.HBM((length, width), f32)] * 2,
        compiler_params=vmem_limit(12),
        name="gate_parts",
    )(me, query, key, value, edge, *taps)

    query_short, skip, spectrum = (
        pltpu.with_memory_space_constraint(a, pltpu.HBM) for a in (query_short, skip, spectrum)
    )

    convolved = pl.pallas_call(
        functools.partial(conv_kernel, (rows, per, lines, devices, group, 4)),
        in_specs=[vmem, hbm] + [vmem] * 5,
        out_specs=vmem,
        out_shape=jax.ShapeDtypeStruct((devices, lines + PAD, LANES), bf16),
        scratch_shapes=[
            pltpu.VMEM((rows * per, LANES), f32),
            pltpu.VMEM((per, rows, 2 * LANES), f32),
            pltpu.SemaphoreType.DMA,
        ],
        compiler_params=vmem_limit(28),
        name="long_conv",
    )(arrived, spectrum, outer, inner, inner_back, outer_back, twist)
    returned = lax.all_to_all(convolved, BOTH, split_axis=0, concat_axis=0, tiled=True)
    returned = returned.reshape(peers, depth, lines + PAD, LANES)

    return pl.pallas_call(
        functools.partial(gate_kernel, (length, per, parts, tiles, count)),
        in_specs=[vmem, hbm, hbm],
        out_specs=hbm,
        out_shape=jax.ShapeDtypeStruct((length, width), f32),
        scratch_shapes=[pltpu.VMEM((length, width), f32)] * 3
        + [pltpu.SemaphoreType.DMA((3, count))],
        compiler_params=vmem_limit(20),
        name="gate",
    )(returned, query_short, skip)


def solution(mesh):
    sizes = (mesh.shape["ctx"], mesh.shape["tp"])
    return jax.shard_map(
        functools.partial(local, sizes),
        mesh=mesh,
        in_specs=(
            P(BOTH, None),
            P(BOTH, None),
            P(BOTH, None),
            P("ctx", "tp"),
            P(None, None, "tp"),
            P("tp"),
        ),
        out_specs=P(BOTH, None),
        check_vma=False,
    )
```

```python
import functools

import jax
import jax.numpy as jnp
import ml_dtypes
import numpy as np
from jax import lax
from jax.experimental import pallas as pl
from jax.experimental.pallas import tpu as pltpu
from jax.sharding import PartitionSpec as P

LANES = 128
PAD = 8
SPAN = 240.0
BOTH = ("ctx", "tp")
bf16, f32 = jnp.bfloat16, jnp.float32


def split_table(table, axis):
    high = table.astype(ml_dtypes.bfloat16)
    low = (table - high.astype(np.float64)).astype(ml_dtypes.bfloat16)
    parts = [high, low, high] if axis == 1 else [high, high, low]
    return np.concatenate(parts, axis)


@functools.lru_cache(maxsize=None)
def transform_tables(rows):
    m = np.arange(rows)
    k1 = np.arange(rows) + 0.5
    b = np.arange(LANES)
    outer = 2.0 * np.pi * np.outer(k1, m) / (2 * rows)
    inner = 2.0 * np.pi * (np.outer(b, b) % LANES) / LANES
    twist = 2.0 * np.pi * np.outer(k1, b) / (2 * LANES * rows)
    c, s = np.cos(inner), np.sin(inner)
    outer_forward = np.concatenate([np.cos(outer), -np.sin(outer)], 0)
    inner_forward = np.block([[c, -s], [s, c]])
    return (
        split_table(outer_forward, 1),
        split_table(inner_forward, 0),
        split_table(inner_forward.T, 0),
        split_table(outer_forward.T, 1),
        np.stack([np.cos(twist), -np.sin(twist)]).astype(np.float32),
    )


def halves(value):
    high = value.astype(bf16)
    return high, (value - high.astype(f32)).astype(bf16)


def from_left(table, value):
    high, low = halves(value)
    return jnp.dot(table[...], jnp.concatenate([high, high, low], 0), preferred_element_type=f32)


def from_right(value, table):
    high, low = halves(value)
    return jnp.dot(jnp.concatenate([high, low, high], 1), table[...], preferred_element_type=f32)


def forward(signal, rows, outer, inner, twist):
    group = signal.shape[1] // LANES
    columns = from_left(outer, signal)
    cos, sin = twist[0], twist[1]
    stacked = []
    for p in range(group):
        re = columns[:rows, p * LANES : (p + 1) * LANES]
        im = columns[rows:, p * LANES : (p + 1) * LANES]
        stacked.append(jnp.concatenate([re * cos - im * sin, re * sin + im * cos], 1))
    return from_right(jnp.concatenate(stacked, 0), inner)


def backward(spectrum, rows, inner, outer, twist):
    group = spectrum.shape[0] // rows
    lines = from_right(spectrum, inner)
    cos, sin = twist[0], twist[1]
    columns = []
    for p in range(group):
        re = lines[p * rows : (p + 1) * rows, :LANES]
        im = lines[p * rows : (p + 1) * rows, LANES:]
        columns.append(jnp.concatenate([re * cos + im * sin, im * cos - re * sin], 0))
    return from_left(outer, jnp.concatenate(columns, 1))


def encode(value, inverse_scale):
    magnitude = jnp.exp2(jnp.abs(value) * inverse_scale * SPAN - SPAN / 2)
    return jnp.where(value < 0, -magnitude, magnitude)


def decode(code, scale):
    magnitude = (jnp.log2(jnp.abs(code)) + SPAN / 2) * (scale * (1.0 / SPAN))
    return jnp.where(code < 0, -magnitude, magnitude)


def block_scale(largest):
    return jnp.maximum(largest * 1.0078125, 1e-30).astype(bf16).astype(f32)


def short_conv(ext_ref, weights, length):
    return (
        weights[0:1] * ext_ref[8 : 8 + length]
        + weights[1:2] * ext_ref[7 : 7 + length]
        + weights[2:3] * ext_ref[6 : 6 + length]
    )


def fill(ext_ref, current, before):
    ext_ref[6:8] = before
    ext_ref[8 : 8 + current.shape[0]] = current.astype(f32)


def columns(j):
    return pl.ds(pl.multiple_of(j * LANES, LANES), LANES)


def lane_index(shape):
    return lax.broadcasted_iota(jnp.int32, shape, 1)


def edges_kernel(q_ref, k_ref, v_ref, short_ref, skip_ref, edge_ref, own_ref, rows_ref):
    last = q_ref.shape[0]
    shard = own_ref.shape[1]
    rows_ref[...] = jnp.zeros_like(rows_ref)
    own_ref[0:6] = jnp.zeros((6, shard), f32)
    for i, ref in enumerate((q_ref, k_ref, v_ref)):
        rows_ref[2 * i : 2 * i + 2] = ref[...].astype(f32)[last - 2 : last]
        own_ref[6 + 3 * i : 9 + 3 * i] = short_ref[i]
    own_ref[15:16] = skip_ref[...]
    rest = own_ref[6:16]
    for i in range(3):
        part = rest.astype(bf16).astype(f32)
        rows_ref[6:16, i * shard : (i + 1) * shard] = part
        rest = rest - part
    edge_ref[...] = rows_ref[...].astype(bf16)


def taps_and_edge(idx_ref, refs, tiles, j):
    edge_ref, *held = refs
    depth = len(held) + 1
    behind = lax.rem(idx_ref[1] - j // tiles + depth, depth)
    tile = lax.rem(j, tiles)
    parts = [edge_ref[:, columns(tile + i * tiles)].astype(f32) for i in range(3)]
    taps = jnp.where(behind == 1, parts[0] + parts[1] + parts[2], held[0][:, columns(tile)])
    for s in range(2, depth):
        taps = jnp.where(behind == s, held[s - 1][:, columns(tile)], taps)
    first = (idx_ref[0] == 0) & (idx_ref[1] == 0)
    before = edge_ref[:, columns(j)].astype(f32)[0:6]
    return taps[6:15], taps[15:16], jnp.where(first, 0.0, before)


def column_copies(sources, targets, sems, j):
    return [
        pltpu.make_async_copy(s.at[:, columns(j)], t.at[:, columns(j)], sems.at[i, j])
        for i, (s, t) in enumerate(zip(sources, targets))
    ]


def start_all(copies_of, count):
    def step(j, carry):
        for copy in copies_of(j):
            copy.start()
        return carry

    lax.fori_loop(0, count, step, 0)


def wait_all(copies_of, count):
    def step(j, carry):
        for copy in copies_of(j):
            copy.wait()
        return carry

    lax.fori_loop(0, count, step, 0)


def rows_out_kernel(dims, idx_ref, k_hbm, v_hbm, *refs):
    length, per, parts, tiles, count = dims
    out_hbm, k_ref, v_ref, out_ref, k_ext, v_ext, sems, out_sems = refs[-8:]
    steps = length // LANES
    into = lambda j: column_copies((k_hbm, v_hbm), (k_ref, v_ref), sems, j)
    start_all(into, count)

    def out_of(j):
        where = (pl.ds(lax.rem(j, tiles) * parts, parts), pl.ds(j // tiles, 1))
        return [pltpu.make_async_copy(out_ref.at[where], out_hbm.at[where], out_sems.at[j])]

    def tile(j, carry):
        weights, _, before = taps_and_edge(idx_ref, refs[:-8], tiles, j)
        for copy in into(j):
            copy.wait()
        fill(k_ext, k_ref[:, columns(j)], before[2:4])
        fill(v_ext, v_ref[:, columns(j)], before[4:6])
        mixed = short_conv(k_ext, weights[3:6], length) * short_conv(v_ext, weights[6:9], length)
        codes, scales = [], []
        for step in range(steps):
            block = mixed[step * LANES : (step + 1) * LANES]
            scale = block_scale(jnp.max(jnp.abs(block), 0, keepdims=True))
            scales.append(scale)
            codes.append(encode(block, 1.0 / scale).astype(bf16).T.astype(f32))
        unused = [jnp.ones((PAD - steps, LANES), f32)]
        lines = jnp.concatenate([*scales, *unused], 0)
        for g in range(parts):
            piece = [code[g * per : (g + 1) * per] for code in codes]
            line = pltpu.roll(lines, (-g * per) % LANES, 1)
            whole_piece = jnp.concatenate(piece + [line], 0).astype(bf16)
            out_ref[lax.rem(j, tiles) * parts + g, j // tiles] = whole_piece
        for copy in out_of(j):
            copy.start()
        return carry

    lax.fori_loop(0, count, tile, 0)
    wait_all(out_of, count)


def gate_parts_kernel(dims, idx_ref, q_ref, k_ref, v_ref, *refs):
    length, tiles = dims
    short_ref, skip_ref, q_ext, k_ext, v_ext = refs[-5:]
    weights, bias, before = taps_and_edge(idx_ref, refs[:-5], tiles, pl.program_id(0))
    fill(q_ext, q_ref[...], before[0:2])
    fill(k_ext, k_ref[...], before[2:4])
    fill(v_ext, v_ref[...], before[4:6])
    mixed = short_conv(k_ext, weights[3:6], length) * short_conv(v_ext, weights[6:9], length)
    short_ref[...] = short_conv(q_ext, weights[0:3], length)
    skip_ref[...] = bias * mixed


def gate_kernel(dims, y_ref, short_hbm, skip_hbm, out_hbm, short_ref, skip_ref, out_ref, sems):
    length, per, parts, tiles, count = dims
    steps = length // LANES
    rows = steps * per
    into = lambda j: column_copies((short_hbm, skip_hbm), (short_ref, skip_ref), sems, j)
    out_of = lambda j: column_copies((out_ref,), (out_hbm,), sems.at[pl.ds(2, 1)], j)
    start_all(into, count)

    def tile(j, carry):
        pieces = [
            y_ref[lax.rem(j, tiles) * parts + g, j // tiles].astype(f32) for g in range(parts)
        ]
        lane = lane_index((PAD, LANES))
        moved = [pltpu.roll(pieces[g][rows:], g * per, 1) for g in range(parts)]
        values = []
        for step in range(steps):
            code = jnp.concatenate([t[step * per : (step + 1) * per] for t in pieces], 0).T
            scale = jnp.ones((PAD, LANES), f32)
            for g in range(parts):
                inside = (lane >= g * per) & (lane < (g + 1) * per)
                scale = jnp.where(inside, moved[g], scale)
            values.append(decode(code, scale[step : step + 1]))
        for copy in into(j):
            copy.wait()
        for step in range(steps):
            here = pl.ds(step * LANES, LANES)
            out_ref[here, columns(j)] = short_ref[here, columns(j)] * (
                values[step] + skip_ref[here, columns(j)]
            )
        for copy in out_of(j):
            copy.start()
        return carry

    lax.fori_loop(0, count, tile, 0)
    wait_all(out_of, count)


def filter_rows_kernel(dims, idx_ref, h_ref, *refs):
    per, peers, chunk = dims
    outs, turned, lines = refs[:peers], refs[-2], refs[-1]
    me = idx_ref[0]
    parts = LANES // per
    for r in range(chunk):
        for c in range(h_ref.shape[1] // LANES):
            block = h_ref[r * LANES : (r + 1) * LANES, c * LANES : (c + 1) * LANES]
            scale = block_scale(jnp.max(jnp.abs(block), 0, keepdims=True))
            code = encode(block, 1.0 / scale).T.astype(bf16)
            wide = jnp.broadcast_to(scale, (PAD, LANES))
            for g in range(parts):
                turned[c * parts + g, r] = code[g * per : (g + 1) * per]
                lines[c * parts + g, r : r + 1] = pltpu.roll(wide, (-g * per) % LANES, 1)[0:1]
    for s in range(peers):
        peer = lax.bitwise_xor(me, s)
        outs[s][0 : chunk * per] = turned[peer].reshape(chunk * per, LANES)
        outs[s][chunk * per :] = lines[peer].astype(bf16)


def filter_kernel(dims, idx_ref, *refs):
    rows, per, peers, group = dims
    pieces = refs[:peers]
    outer, inner, twist, out_hbm, out_ref, coded, scales, held, wide, sems, out_sems = refs[peers:]
    me = idx_ref[0]
    chunk = rows // peers
    size = chunk * per
    copies = []
    for s in range(peers):
        peer = lax.bitwise_xor(me, s)
        copies.append(
            pltpu.make_async_copy(
                pieces[s].at[pl.ds(0, size)],
                coded.at[pl.ds(pl.multiple_of(peer * size, 16), size)],
                sems.at[0, s],
            )
        )
        copies.append(
            pltpu.make_async_copy(
                pieces[s].at[pl.ds(size, chunk)],
                scales.at[pl.ds(pl.multiple_of(peer * chunk, 16), chunk)],
                sems.at[1, s],
            )
        )
    for copy in copies:
        copy.start()
    for copy in copies:
        copy.wait()
    wide[...] = scales[...].astype(f32)

    def out_of(i):
        where = pl.ds(i * group, group)
        return [pltpu.make_async_copy(out_ref.at[where], out_hbm.at[where], out_sems.at[i])]

    def widen(i, carry):
        here = pl.ds(pl.multiple_of(i * size, 16), size)
        held[here, :] = coded[here, :].astype(f32)
        return carry

    lax.fori_loop(0, peers, widen, 0)

    def body(i):
        first = i * group
        near = pltpu.roll(wide[...], LANES - first, 1)
        signal = jnp.concatenate(
            [
                decode(held[pl.ds(first + p, rows, stride=per), :], near[:, p : p + 1])
                for p in range(group)
            ],
            1,
        )
        spectrum = forward(signal, rows, outer, inner, twist) * (1.0 / (LANES * rows))
        for p in range(group):
            out_ref[first + p] = spectrum[p * rows : (p + 1) * rows]
        for copy in out_of(i):
            copy.start()

    for i in range(per // group):
        body(i)
    wait_all(out_of, per // group)


def conv_kernel(
    dims, x_ref, h_hbm, outer, inner, inner_back, outer_back, twist, out_ref, *scratch
):
    rows, per, lines, blocks, group, batch = dims
    held, h_ref, scales, found, sems = scratch
    steps = lines // per
    fetches = []
    for i in range(per // group):
        part = pl.ds(i * group, group)
        fetches.append(pltpu.make_async_copy(h_hbm.at[part], h_ref.at[part], sems.at[i]))
        fetches[-1].start()

    def unpack(i, carry):
        for j in range(batch):
            tile = x_ref[i * batch + j].astype(f32)
            held[pl.ds(pl.multiple_of((i * batch + j) * lines, 8), lines), :] = tile[:lines]
            scales[i * batch + j] = tile[lines : lines + steps]
        return carry

    lax.fori_loop(0, blocks // batch, unpack, 0)
    lane = lane_index((rows, LANES))

    def body(i):
        first = i * group
        near = pltpu.roll(scales[...].reshape(rows, LANES), LANES - first, 1)
        signal = jnp.concatenate(
            [
                decode(held[pl.ds(first + p, rows, stride=per), :], near[:, p : p + 1])
                for p in range(group)
            ],
            1,
        )
        spectrum = forward(signal, rows, outer, inner, twist)
        fetches[i].wait()
        joined = []
        for p in range(group):
            re = spectrum[p * rows : (p + 1) * rows, :LANES]
            im = spectrum[p * rows : (p + 1) * rows, LANES:]
            h_re, h_im = h_ref[first + p, :, :LANES], h_ref[first + p, :, LANES:]
            joined.append(jnp.concatenate([re * h_re - im * h_im, re * h_im + im * h_re], 1))
        result = backward(jnp.concatenate(joined, 0), rows, inner_back, outer_back, twist)
        for p in range(group):
            value = result[:, p * LANES : (p + 1) * LANES]
            scale = block_scale(jnp.max(jnp.abs(value), 1, keepdims=True))
            held[pl.ds(first + p, rows, stride=per), :] = encode(value, 1.0 / scale)
            found[...] = jnp.where(lane == first + p, scale, found[...])

    found[...] = jnp.ones_like(found)
    for i in range(per // group):
        body(i)
    scales[...] = found[...].reshape(scales.shape)

    def pack(i, carry):
        for j in range(batch):
            start = pl.multiple_of((i * batch + j) * lines, 8)
            line = jnp.concatenate([scales[i * batch + j], jnp.ones((PAD - steps, LANES), f32)], 0)
            tile = jnp.concatenate([held[pl.ds(start, lines), :], line], 0)
            out_ref[i * batch + j] = tile.astype(bf16)
        return carry

    lax.fori_loop(0, blocks // batch, pack, 0)


def whole(array):
    return pl.BlockSpec(array.shape, lambda *_: (0,) * len(array.shape))


def vmem_limit(mebibytes):
    return pltpu.CompilerParams(vmem_limit_bytes=mebibytes * 1024 * 1024)


def local(sizes, query, key, value, long_filter, short_filter, skip_bias):
    peers, depth = sizes
    devices = peers * depth
    length, width = query.shape
    shard = long_filter.shape[1]
    per = shard // peers
    rows = length * devices // LANES
    lines = length // LANES * per
    parts = LANES // per
    tiles = shard // LANES
    group = min(8, per)
    me = jnp.stack([lax.axis_index(axis) for axis in BOTH]).astype(jnp.int32)
    tables = transform_tables(rows)
    outer, inner, inner_back, outer_back, twist = (jnp.asarray(t) for t in tables)

    def crossed(array, axis, count):
        return [array[0]] + [
            lax.ppermute(array[s], axis, [(i, i ^ s) for i in range(count)])
            for s in range(1, count)
        ]

    query, key, value = (pltpu.with_memory_space_constraint(a, pltpu.HBM) for a in (query, key, value))
    last = pl.BlockSpec((16, width), lambda i: (length // 16 - 1, 0))
    taps_hbm, bias_hbm = (
        pltpu.with_memory_space_constraint(a, pltpu.HBM)
        for a in (short_filter, skip_bias.reshape(1, shard))
    )
    edge, own = pl.pallas_call(
        edges_kernel,
        grid=(1,),
        in_specs=[last] * 3 + [whole(short_filter), pl.BlockSpec((1, shard), lambda i: (0, 0))],
        out_specs=[
            pl.BlockSpec((16, width), lambda i: (0, 0)),
            pl.BlockSpec((16, shard), lambda i: (0, 0)),
        ],
        out_shape=[
            jax.ShapeDtypeStruct((16, width), bf16),
            jax.ShapeDtypeStruct((16, shard), f32),
        ],
        scratch_shapes=[pltpu.VMEM((16, width), f32)],
        compiler_params=vmem_limit(8),
        name="edges",
    )(query, key, value, taps_hbm, bias_hbm)

    def shifted(array, by):
        return lax.ppermute(array, BOTH, [(i, (i + by) % devices) for i in range(devices)])

    edge = shifted(edge, 1)
    taps = [own] + [shifted(own, s) for s in range(2, depth)]

    chunk = long_filter.shape[0] // LANES
    pieces = pl.pallas_call(
        functools.partial(filter_rows_kernel, (per, peers, chunk)),
        grid_spec=pltpu.PrefetchScalarGridSpec(
            num_scalar_prefetch=1,
            grid=(1,),
            in_specs=[whole(long_filter)],
            out_specs=[pl.BlockSpec((chunk * per + chunk, LANES), lambda *_: (0, 0))] * peers,
            scratch_shapes=[
                pltpu.VMEM((peers, chunk, per, LANES), bf16),
                pltpu.VMEM((peers, chunk, LANES), f32),
            ],
        ),
        out_shape=[pltpu.HBM((chunk * per + chunk, LANES), bf16)] * peers,
        compiler_params=vmem_limit(16),
        name="filter_rows",
    )(me, long_filter)
    pieces = list(pieces)
    early = [s for s in (2, 4) if s < peers]
    edge, *ready = lax.optimization_barrier((edge, *taps[1:], *(pieces[s] for s in early)))
    taps[1:] = ready[: depth - 2]
    for s, piece in zip(early, ready[depth - 2 :]):
        pieces[s] = piece
    pieces = crossed(pieces, "ctx", peers)

    row_spec = pl.BlockSpec((length, LANES), lambda j, _: (0, j))
    wire_shape = jax.ShapeDtypeStruct((peers, depth, lines + PAD, LANES), bf16)
    ext = pltpu.VMEM((length + 8, LANES), f32)
    vmem, hbm = pl.BlockSpec(memory_space=pltpu.VMEM), pl.BlockSpec(memory_space=pltpu.HBM)
    count = width // LANES
    coded = pl.pallas_call(
        functools.partial(rows_out_kernel, (length, per, parts, tiles, count)),
        in_specs=[pl.BlockSpec(memory_space=pltpu.SMEM), hbm, hbm] + [vmem] * depth,
        out_specs=hbm,
        out_shape=wire_shape,
        scratch_shapes=[
            pltpu.VMEM((length, width), bf16),
            pltpu.VMEM((length, width), bf16),
            pltpu.VMEM(wire_shape.shape, bf16),
            ext,
            ext,
            pltpu.SemaphoreType.DMA((2, count)),
            pltpu.SemaphoreType.DMA((count,)),
        ],
        compiler_params=vmem_limit(16),
        name="mixed_rows",
    )(me, key, value, edge, *taps)
    coded, *ready = lax.optimization_barrier((coded, *(pieces[s] for s in early)))
    for s, piece in zip(early, ready):
        pieces[s] = piece
    coded = coded.reshape(devices, lines + PAD, LANES)
    arrived = lax.all_to_all(coded, BOTH, split_axis=0, concat_axis=0, tiled=True)

    spectrum = pl.pallas_call(
        functools.partial(filter_kernel, (rows, per, peers, group)),
        grid_spec=pltpu.PrefetchScalarGridSpec(
            num_scalar_prefetch=1,
            grid=(1,),
            in_specs=[pl.BlockSpec(memory_space=pltpu.HBM)] * peers
            + [whole(outer), whole(inner), whole(twist)],
            out_specs=hbm,
            scratch_shapes=[
                pltpu.VMEM((per, rows, 2 * LANES), f32),
                pltpu.VMEM((rows * per, LANES), bf16),
                pltpu.VMEM((rows, LANES), bf16),
                pltpu.VMEM((rows * per, LANES), f32),
                pltpu.VMEM((rows, LANES), f32),
                pltpu.SemaphoreType.DMA((2, peers)),
                pltpu.SemaphoreType.DMA((per // group,)),
            ],
        ),
        out_shape=pltpu.HBM((per, rows, 2 * LANES), f32),
        compiler_params=vmem_limit(28),
        name="filter_spectrum",
    )(me, *pieces, outer, inner, twist)

    query_short, skip = pl.pallas_call(
        functools.partial(gate_parts_kernel, (length, tiles)),
        grid_spec=pltpu.PrefetchScalarGridSpec(
            num_scalar_prefetch=1,
            grid=(width // LANES,),
            in_specs=[row_spec] * 3 + [whole(edge)] + [whole(tap) for tap in taps],
            out_specs=[row_spec, row_spec],
            scratch_shapes=[ext] * 3,
        ),
        out_shape=[pltpu.HBM((length, width), f32)] * 2,
        compiler_params=vmem_limit(12),
        name="gate_parts",
    )(me, query, key, value, edge, *taps)

    query_short, skip, spectrum = (
        pltpu.with_memory_space_constraint(a, pltpu.HBM) for a in (query_short, skip, spectrum)
    )

    convolved = pl.pallas_call(
        functools.partial(conv_kernel, (rows, per, lines, devices, group, 8)),
        in_specs=[vmem, hbm] + [vmem] * 5,
        out_specs=vmem,
        out_shape=jax.ShapeDtypeStruct((devices, lines + PAD, LANES), bf16),
        scratch_shapes=[
            pltpu.VMEM((rows * per, LANES), f32),
            pltpu.VMEM((per, rows, 2 * LANES), f32),
            pltpu.VMEM((devices, length // LANES, LANES), f32),
            pltpu.VMEM((rows, LANES), f32),
            pltpu.SemaphoreType.DMA((per // group,)),
        ],
        compiler_params=vmem_limit(28),
        name="long_conv",
    )(arrived, spectrum, outer, inner, inner_back, outer_back, twist)
    returned = lax.all_to_all(convolved, BOTH, split_axis=0, concat_axis=0, tiled=True)
    returned = returned.reshape(peers, depth, lines + PAD, LANES)

    return pl.pallas_call(
        functools.partial(gate_kernel, (length, per, parts, tiles, count)),
        in_specs=[vmem, hbm, hbm],
        out_specs=hbm,
        out_shape=jax.ShapeDtypeStruct((length, width), f32),
        scratch_shapes=[pltpu.VMEM((length, width), f32)] * 3
        + [pltpu.SemaphoreType.DMA((3, count))],
        compiler_params=vmem_limit(20),
        name="gate",
    )(returned, query_short, skip)


def solution(mesh):
    sizes = (mesh.shape["ctx"], mesh.shape["tp"])
    return jax.shard_map(
        functools.partial(local, sizes),
        mesh=mesh,
        in_specs=(
            P(BOTH, None),
            P(BOTH, None),
            P(BOTH, None),
            P("ctx", "tp"),
            P(None, None, "tp"),
            P("tp"),
        ),
        out_specs=P(BOTH, None),
        check_vma=False,
    )
```

```python
import functools

import jax
import jax.numpy as jnp
import ml_dtypes
import numpy as np
from jax import lax
from jax.experimental import pallas as pl
from jax.experimental.pallas import tpu as pltpu
from jax.sharding import PartitionSpec as P

LANES = 128
PAD = 8
SPAN = 240.0
BOTH = ("ctx", "tp")
bf16, f32 = jnp.bfloat16, jnp.float32


def split_table(table, axis):
    high = table.astype(ml_dtypes.bfloat16)
    low = (table - high.astype(np.float64)).astype(ml_dtypes.bfloat16)
    parts = [high, low, high] if axis == 1 else [high, high, low]
    return np.concatenate(parts, axis)


@functools.lru_cache(maxsize=None)
def transform_tables(rows):
    m = np.arange(rows)
    k1 = np.arange(rows) + 0.5
    b = np.arange(LANES)
    outer = 2.0 * np.pi * np.outer(k1, m) / (2 * rows)
    inner = 2.0 * np.pi * (np.outer(b, b) % LANES) / LANES
    twist = 2.0 * np.pi * np.outer(k1, b) / (2 * LANES * rows)
    c, s = np.cos(inner), np.sin(inner)
    outer_forward = np.concatenate([np.cos(outer), -np.sin(outer)], 0)
    inner_forward = np.block([[c, -s], [s, c]])
    return (
        split_table(outer_forward, 1),
        split_table(inner_forward, 0),
        split_table(inner_forward.T, 0),
        split_table(outer_forward.T, 1),
        np.stack([np.cos(twist), -np.sin(twist)]).astype(np.float32),
    )


def halves(value):
    high = value.astype(bf16)
    return high, (value - high.astype(f32)).astype(bf16)


def from_left(table, value):
    high, low = halves(value)
    return jnp.dot(table[...], jnp.concatenate([high, high, low], 0), preferred_element_type=f32)


def from_right(value, table):
    high, low = halves(value)
    return jnp.dot(jnp.concatenate([high, low, high], 1), table[...], preferred_element_type=f32)


def forward(signal, rows, outer, inner, twist):
    group = signal.shape[1] // LANES
    columns = from_left(outer, signal)
    cos, sin = twist[0], twist[1]
    stacked = []
    for p in range(group):
        re = columns[:rows, p * LANES : (p + 1) * LANES]
        im = columns[rows:, p * LANES : (p + 1) * LANES]
        stacked.append(jnp.concatenate([re * cos - im * sin, re * sin + im * cos], 1))
    return from_right(jnp.concatenate(stacked, 0), inner)


def backward(spectrum, rows, inner, outer, twist):
    group = spectrum.shape[0] // rows
    lines = from_right(spectrum, inner)
    cos, sin = twist[0], twist[1]
    columns = []
    for p in range(group):
        re = lines[p * rows : (p + 1) * rows, :LANES]
        im = lines[p * rows : (p + 1) * rows, LANES:]
        columns.append(jnp.concatenate([re * cos + im * sin, im * cos - re * sin], 0))
    return from_left(outer, jnp.concatenate(columns, 1))


def encode(value, inverse_scale):
    magnitude = jnp.exp2(jnp.abs(value) * inverse_scale * SPAN - SPAN / 2)
    return jnp.where(value < 0, -magnitude, magnitude)


def decode(code, scale):
    magnitude = (jnp.log2(jnp.abs(code)) + SPAN / 2) * (scale * (1.0 / SPAN))
    return jnp.where(code < 0, -magnitude, magnitude)


def block_scale(largest):
    return jnp.maximum(largest * 1.0078125, 1e-30).astype(bf16).astype(f32)


def short_conv(ext_ref, weights, length):
    return (
        weights[0:1] * ext_ref[8 : 8 + length]
        + weights[1:2] * ext_ref[7 : 7 + length]
        + weights[2:3] * ext_ref[6 : 6 + length]
    )


def fill(ext_ref, current, before):
    ext_ref[6:8] = before
    ext_ref[8 : 8 + current.shape[0]] = current.astype(f32)


def columns(j):
    return pl.ds(pl.multiple_of(j * LANES, LANES), LANES)


def lane_index(shape):
    return lax.broadcasted_iota(jnp.int32, shape, 1)


def edges_kernel(q_ref, k_ref, v_ref, short_ref, skip_ref, edge_ref, own_ref, rows_ref):
    last = q_ref.shape[0]
    shard = own_ref.shape[1]
    rows_ref[...] = jnp.zeros_like(rows_ref)
    own_ref[0:6] = jnp.zeros((6, shard), f32)
    for i, ref in enumerate((q_ref, k_ref, v_ref)):
        rows_ref[2 * i : 2 * i + 2] = ref[...].astype(f32)[last - 2 : last]
        own_ref[6 + 3 * i : 9 + 3 * i] = short_ref[i]
    own_ref[15:16] = skip_ref[...]
    rest = own_ref[6:16]
    for i in range(3):
        part = rest.astype(bf16).astype(f32)
        rows_ref[6:16, i * shard : (i + 1) * shard] = part
        rest = rest - part
    edge_ref[...] = rows_ref[...].astype(bf16)


def taps_and_edge(idx_ref, refs, tiles, j):
    edge_ref, *held = refs
    depth = len(held) + 1
    behind = lax.rem(idx_ref[1] - j // tiles + depth, depth)
    tile = lax.rem(j, tiles)
    parts = [edge_ref[:, columns(tile + i * tiles)].astype(f32) for i in range(3)]
    taps = jnp.where(behind == 1, parts[0] + parts[1] + parts[2], held[0][:, columns(tile)])
    for s in range(2, depth):
        taps = jnp.where(behind == s, held[s - 1][:, columns(tile)], taps)
    first = (idx_ref[0] == 0) & (idx_ref[1] == 0)
    before = edge_ref[:, columns(j)].astype(f32)[0:6]
    return taps[6:15], taps[15:16], jnp.where(first, 0.0, before)


def column_copies(sources, targets, sems, j):
    return [
        pltpu.make_async_copy(s.at[:, columns(j)], t.at[:, columns(j)], sems.at[i, j])
        for i, (s, t) in enumerate(zip(sources, targets))
    ]


def start_all(copies_of, count):
    def step(j, carry):
        for copy in copies_of(j):
            copy.start()
        return carry

    lax.fori_loop(0, count, step, 0)


def wait_all(copies_of, count):
    def step(j, carry):
        for copy in copies_of(j):
            copy.wait()
        return carry

    lax.fori_loop(0, count, step, 0)


def rows_out_kernel(dims, idx_ref, k_ref, v_ref, *refs):
    length, per, parts, tiles, count = dims
    out_hbm, out_ref, k_ext, v_ext, out_sems = refs[-5:]
    steps = length // LANES

    def out_of(j):
        where = (pl.ds(lax.rem(j, tiles) * parts, parts), pl.ds(j // tiles, 1))
        return [pltpu.make_async_copy(out_ref.at[where], out_hbm.at[where], out_sems.at[j])]

    def tile(j, carry):
        weights, _, before = taps_and_edge(idx_ref, refs[:-5], tiles, j)
        fill(k_ext, k_ref[:, columns(j)], before[2:4])
        fill(v_ext, v_ref[:, columns(j)], before[4:6])
        mixed = short_conv(k_ext, weights[3:6], length) * short_conv(v_ext, weights[6:9], length)
        codes, scales = [], []
        for step in range(steps):
            block = mixed[step * LANES : (step + 1) * LANES]
            scale = block_scale(jnp.max(jnp.abs(block), 0, keepdims=True))
            scales.append(scale)
            codes.append(encode(block, 1.0 / scale).astype(bf16).T.astype(f32))
        unused = [jnp.ones((PAD - steps, LANES), f32)]
        lines = jnp.concatenate([*scales, *unused], 0)
        for g in range(parts):
            piece = [code[g * per : (g + 1) * per] for code in codes]
            line = pltpu.roll(lines, (-g * per) % LANES, 1)
            whole_piece = jnp.concatenate(piece + [line], 0).astype(bf16)
            out_ref[lax.rem(j, tiles) * parts + g, j // tiles] = whole_piece
        for copy in out_of(j):
            copy.start()
        return carry

    lax.fori_loop(0, count, tile, 0)
    wait_all(out_of, count)


def gate_parts_kernel(dims, idx_ref, q_ref, k_ref, v_ref, *refs):
    length, tiles = dims
    short_ref, skip_ref, q_ext, k_ext, v_ext = refs[-5:]
    weights, bias, before = taps_and_edge(idx_ref, refs[:-5], tiles, pl.program_id(0))
    fill(q_ext, q_ref[...], before[0:2])
    fill(k_ext, k_ref[...], before[2:4])
    fill(v_ext, v_ref[...], before[4:6])
    mixed = short_conv(k_ext, weights[3:6], length) * short_conv(v_ext, weights[6:9], length)
    short_ref[...] = short_conv(q_ext, weights[0:3], length)
    skip_ref[...] = bias * mixed


def gate_kernel(dims, y_ref, short_ref, skip_hbm, out_hbm, skip_ref, out_ref, sems, out_sems):
    length, per, parts, tiles, count = dims
    steps = length // LANES
    rows = steps * per
    into = lambda j: column_copies((skip_hbm,), (skip_ref,), sems, j)
    out_of = lambda j: column_copies((out_ref,), (out_hbm,), out_sems, j)
    start_all(into, count)

    def tile(j, carry):
        pieces = [
            y_ref[lax.rem(j, tiles) * parts + g, j // tiles].astype(f32) for g in range(parts)
        ]
        lane = lane_index((PAD, LANES))
        moved = [pltpu.roll(pieces[g][rows:], g * per, 1) for g in range(parts)]
        values = []
        for step in range(steps):
            code = jnp.concatenate([t[step * per : (step + 1) * per] for t in pieces], 0).T
            scale = jnp.ones((PAD, LANES), f32)
            for g in range(parts):
                inside = (lane >= g * per) & (lane < (g + 1) * per)
                scale = jnp.where(inside, moved[g], scale)
            values.append(decode(code, scale[step : step + 1]))
        for copy in into(j):
            copy.wait()
        for step in range(steps):
            here = pl.ds(step * LANES, LANES)
            out_ref[here, columns(j)] = short_ref[here, columns(j)] * (
                values[step] + skip_ref[here, columns(j)]
            )
        for copy in out_of(j):
            copy.start()
        return carry

    lax.fori_loop(0, count, tile, 0)
    wait_all(out_of, count)


def filter_rows_kernel(dims, idx_ref, h_ref, k_hbm, v_hbm, *refs):
    per, peers, chunk = dims
    outs, (k_ref, v_ref, turned, lines, sems) = refs[:peers], refs[peers:]
    fetches = [
        pltpu.make_async_copy(k_hbm, k_ref, sems.at[0]),
        pltpu.make_async_copy(v_hbm, v_ref, sems.at[1]),
    ]
    for fetch in fetches:
        fetch.start()
    me = idx_ref[0]
    parts = LANES // per
    for r in range(chunk):
        for c in range(h_ref.shape[1] // LANES):
            block = h_ref[r * LANES : (r + 1) * LANES, c * LANES : (c + 1) * LANES]
            scale = block_scale(jnp.max(jnp.abs(block), 0, keepdims=True))
            code = encode(block, 1.0 / scale).T.astype(bf16)
            wide = jnp.broadcast_to(scale, (PAD, LANES))
            for g in range(parts):
                turned[c * parts + g, r] = code[g * per : (g + 1) * per]
                lines[c * parts + g, r : r + 1] = pltpu.roll(wide, (-g * per) % LANES, 1)[0:1]
    for s in range(peers):
        peer = lax.bitwise_xor(me, s)
        outs[s][0 : chunk * per] = turned[peer].reshape(chunk * per, LANES)
        outs[s][chunk * per :] = lines[peer].astype(bf16)
    for fetch in fetches:
        fetch.wait()


def filter_kernel(dims, idx_ref, *refs):
    rows, per, peers, group = dims
    pieces = refs[:peers]
    outer, inner, twist, out_hbm, out_ref, coded, scales, held, wide, sems, out_sems = refs[peers:]
    me = idx_ref[0]
    chunk = rows // peers
    size = chunk * per
    copies = []
    for s in range(peers):
        peer = lax.bitwise_xor(me, s)
        copies.append(
            pltpu.make_async_copy(
                pieces[s].at[pl.ds(0, size)],
                coded.at[pl.ds(pl.multiple_of(peer * size, 16), size)],
                sems.at[0, s],
            )
        )
        copies.append(
            pltpu.make_async_copy(
                pieces[s].at[pl.ds(size, chunk)],
                scales.at[pl.ds(pl.multiple_of(peer * chunk, 16), chunk)],
                sems.at[1, s],
            )
        )
    for copy in copies:
        copy.start()
    for copy in copies:
        copy.wait()
    wide[...] = scales[...].astype(f32)

    def out_of(i):
        where = pl.ds(i * group, group)
        return [pltpu.make_async_copy(out_ref.at[where], out_hbm.at[where], out_sems.at[i])]

    def widen(i, carry):
        here = pl.ds(pl.multiple_of(i * size, 16), size)
        held[here, :] = coded[here, :].astype(f32)
        return carry

    lax.fori_loop(0, peers, widen, 0)

    def body(i):
        first = i * group
        near = pltpu.roll(wide[...], LANES - first, 1)
        signal = jnp.concatenate(
            [
                decode(held[pl.ds(first + p, rows, stride=per), :], near[:, p : p + 1])
                for p in range(group)
            ],
            1,
        )
        spectrum = forward(signal, rows, outer, inner, twist) * (1.0 / (LANES * rows))
        for p in range(group):
            out_ref[first + p] = spectrum[p * rows : (p + 1) * rows]
        for copy in out_of(i):
            copy.start()

    for i in range(per // group):
        body(i)
    wait_all(out_of, per // group)


def conv_kernel(
    dims, x_ref, h_hbm, outer, inner, inner_back, outer_back, twist, out_ref, *scratch
):
    rows, per, lines, blocks, group, batch = dims
    held, h_ref, scales, found, sems = scratch
    steps = lines // per
    fetches = []
    for i in range(per // group):
        part = pl.ds(i * group, group)
        fetches.append(pltpu.make_async_copy(h_hbm.at[part], h_ref.at[part], sems.at[i]))
        fetches[-1].start()

    def unpack(i, carry):
        for j in range(batch):
            tile = x_ref[i * batch + j].astype(f32)
            held[pl.ds(pl.multiple_of((i * batch + j) * lines, 8), lines), :] = tile[:lines]
            scales[i * batch + j] = tile[lines : lines + steps]
        return carry

    lax.fori_loop(0, blocks // batch, unpack, 0)
    lane = lane_index((rows, LANES))

    def body(i):
        first = i * group
        near = pltpu.roll(scales[...].reshape(rows, LANES), LANES - first, 1)
        signal = jnp.concatenate(
            [
                decode(held[pl.ds(first + p, rows, stride=per), :], near[:, p : p + 1])
                for p in range(group)
            ],
            1,
        )
        spectrum = forward(signal, rows, outer, inner, twist)
        fetches[i].wait()
        joined = []
        for p in range(group):
            re = spectrum[p * rows : (p + 1) * rows, :LANES]
            im = spectrum[p * rows : (p + 1) * rows, LANES:]
            h_re, h_im = h_ref[first + p, :, :LANES], h_ref[first + p, :, LANES:]
            joined.append(jnp.concatenate([re * h_re - im * h_im, re * h_im + im * h_re], 1))
        result = backward(jnp.concatenate(joined, 0), rows, inner_back, outer_back, twist)
        for p in range(group):
            value = result[:, p * LANES : (p + 1) * LANES]
            scale = block_scale(jnp.max(jnp.abs(value), 1, keepdims=True))
            held[pl.ds(first + p, rows, stride=per), :] = encode(value, 1.0 / scale)
            found[...] = jnp.where(lane == first + p, scale, found[...])

    found[...] = jnp.ones_like(found)
    for i in range(per // group):
        body(i)
    scales[...] = found[...].reshape(scales.shape)

    def pack(i, carry):
        for j in range(batch):
            start = pl.multiple_of((i * batch + j) * lines, 8)
            line = jnp.concatenate([scales[i * batch + j], jnp.ones((PAD - steps, LANES), f32)], 0)
            tile = jnp.concatenate([held[pl.ds(start, lines), :], line], 0)
            out_ref[i * batch + j] = tile.astype(bf16)
        return carry

    lax.fori_loop(0, blocks // batch, pack, 0)


def whole(array):
    return pl.BlockSpec(array.shape, lambda *_: (0,) * len(array.shape))


def vmem_limit(mebibytes):
    return pltpu.CompilerParams(vmem_limit_bytes=mebibytes * 1024 * 1024)


def local(sizes, query, key, value, long_filter, short_filter, skip_bias):
    peers, depth = sizes
    devices = peers * depth
    length, width = query.shape
    shard = long_filter.shape[1]
    per = shard // peers
    rows = length * devices // LANES
    lines = length // LANES * per
    parts = LANES // per
    tiles = shard // LANES
    group = min(8, per)
    me = jnp.stack([lax.axis_index(axis) for axis in BOTH]).astype(jnp.int32)
    tables = transform_tables(rows)
    outer, inner, inner_back, outer_back, twist = (jnp.asarray(t) for t in tables)

    def crossed(array, axis, count):
        return [array[0]] + [
            lax.ppermute(array[s], axis, [(i, i ^ s) for i in range(count)])
            for s in range(1, count)
        ]

    query, key, value = (pltpu.with_memory_space_constraint(a, pltpu.HBM) for a in (query, key, value))
    last = pl.BlockSpec((16, width), lambda i: (length // 16 - 1, 0))
    taps_hbm, bias_hbm = (
        pltpu.with_memory_space_constraint(a, pltpu.HBM)
        for a in (short_filter, skip_bias.reshape(1, shard))
    )
    edge, own = pl.pallas_call(
        edges_kernel,
        grid=(1,),
        in_specs=[last] * 3 + [whole(short_filter), pl.BlockSpec((1, shard), lambda i: (0, 0))],
        out_specs=[
            pl.BlockSpec((16, width), lambda i: (0, 0)),
            pl.BlockSpec((16, shard), lambda i: (0, 0)),
        ],
        out_shape=[
            jax.ShapeDtypeStruct((16, width), bf16),
            jax.ShapeDtypeStruct((16, shard), f32),
        ],
        scratch_shapes=[pltpu.VMEM((16, width), f32)],
        compiler_params=vmem_limit(8),
        name="edges",
    )(query, key, value, taps_hbm, bias_hbm)

    def shifted(array, by):
        return lax.ppermute(array, BOTH, [(i, (i + by) % devices) for i in range(devices)])

    edge = shifted(edge, 1)
    taps = [own] + [shifted(own, s) for s in range(2, depth)]

    chunk = long_filter.shape[0] // LANES
    vmem, hbm = pl.BlockSpec(memory_space=pltpu.VMEM), pl.BlockSpec(memory_space=pltpu.HBM)
    *pieces, key_near, value_near = pl.pallas_call(
        functools.partial(filter_rows_kernel, (per, peers, chunk)),
        grid_spec=pltpu.PrefetchScalarGridSpec(
            num_scalar_prefetch=1,
            grid=(1,),
            in_specs=[whole(long_filter), hbm, hbm],
            out_specs=[pl.BlockSpec((chunk * per + chunk, LANES), lambda *_: (0, 0))] * peers
            + [vmem] * 2,
            scratch_shapes=[
                pltpu.VMEM((peers, chunk, per, LANES), bf16),
                pltpu.VMEM((peers, chunk, LANES), f32),
                pltpu.SemaphoreType.DMA((2,)),
            ],
        ),
        out_shape=[pltpu.HBM((chunk * per + chunk, LANES), bf16)] * peers
        + [pltpu.VMEM((length, width), bf16)] * 2,
        compiler_params=vmem_limit(16),
        name="filter_rows",
    )(me, long_filter, key, value)
    pieces = list(pieces)
    early = [s for s in (2, 4, 6) if s < peers]
    edge, *ready = lax.optimization_barrier((edge, *taps[1:], *(pieces[s] for s in early)))
    taps[1:] = ready[: depth - 2]
    for s, piece in zip(early, ready[depth - 2 :]):
        pieces[s] = piece
    pieces = crossed(pieces, "ctx", peers)

    row_spec = pl.BlockSpec((length, LANES), lambda j, _: (0, j))
    wire_shape = jax.ShapeDtypeStruct((peers, depth, lines + PAD, LANES), bf16)
    ext = pltpu.VMEM((length + 8, LANES), f32)
    count = width // LANES
    coded = pl.pallas_call(
        functools.partial(rows_out_kernel, (length, per, parts, tiles, count)),
        in_specs=[pl.BlockSpec(memory_space=pltpu.SMEM)] + [vmem] * (depth + 2),
        out_specs=hbm,
        out_shape=wire_shape,
        scratch_shapes=[
            pltpu.VMEM(wire_shape.shape, bf16),
            ext,
            ext,
            pltpu.SemaphoreType.DMA((count,)),
        ],
        compiler_params=vmem_limit(16),
        name="mixed_rows",
    )(me, key_near, value_near, edge, *taps)
    coded, *ready = lax.optimization_barrier((coded, *(pieces[s] for s in early)))
    for s, piece in zip(early, ready):
        pieces[s] = piece
    coded = coded.reshape(devices, lines + PAD, LANES)
    arrived = lax.all_to_all(coded, BOTH, split_axis=0, concat_axis=0, tiled=True)

    spectrum = pl.pallas_call(
        functools.partial(filter_kernel, (rows, per, peers, group)),
        grid_spec=pltpu.PrefetchScalarGridSpec(
            num_scalar_prefetch=1,
            grid=(1,),
            in_specs=[pl.BlockSpec(memory_space=pltpu.HBM)] * peers
            + [whole(outer), whole(inner), whole(twist)],
            out_specs=hbm,
            scratch_shapes=[
                pltpu.VMEM((per, rows, 2 * LANES), f32),
                pltpu.VMEM((rows * per, LANES), bf16),
                pltpu.VMEM((rows, LANES), bf16),
                pltpu.VMEM((rows * per, LANES), f32),
                pltpu.VMEM((rows, LANES), f32),
                pltpu.SemaphoreType.DMA((2, peers)),
                pltpu.SemaphoreType.DMA((per // group,)),
            ],
        ),
        out_shape=pltpu.HBM((per, rows, 2 * LANES), f32),
        compiler_params=vmem_limit(28),
        name="filter_spectrum",
    )(me, *pieces, outer, inner, twist)

    query_short, skip = pl.pallas_call(
        functools.partial(gate_parts_kernel, (length, tiles)),
        grid_spec=pltpu.PrefetchScalarGridSpec(
            num_scalar_prefetch=1,
            grid=(width // LANES,),
            in_specs=[row_spec] * 3 + [whole(edge)] + [whole(tap) for tap in taps],
            out_specs=[row_spec, row_spec],
            scratch_shapes=[ext] * 3,
        ),
        out_shape=[pltpu.VMEM((length, width), f32), pltpu.HBM((length, width), f32)],
        compiler_params=vmem_limit(12),
        name="gate_parts",
    )(me, query, key, value, edge, *taps)

    skip, spectrum = (pltpu.with_memory_space_constraint(a, pltpu.HBM) for a in (skip, spectrum))

    convolved = pl.pallas_call(
        functools.partial(conv_kernel, (rows, per, lines, devices, group, 8)),
        in_specs=[vmem, hbm] + [vmem] * 5,
        out_specs=vmem,
        out_shape=jax.ShapeDtypeStruct((devices, lines + PAD, LANES), bf16),
        scratch_shapes=[
            pltpu.VMEM((rows * per, LANES), f32),
            pltpu.VMEM((per, rows, 2 * LANES), f32),
            pltpu.VMEM((devices, length // LANES, LANES), f32),
            pltpu.VMEM((rows, LANES), f32),
            pltpu.SemaphoreType.DMA((per // group,)),
        ],
        compiler_params=vmem_limit(28),
        name="long_conv",
    )(arrived, spectrum, outer, inner, inner_back, outer_back, twist)
    returned = lax.all_to_all(convolved, BOTH, split_axis=0, concat_axis=0, tiled=True)
    returned = returned.reshape(peers, depth, lines + PAD, LANES)

    return pl.pallas_call(
        functools.partial(gate_kernel, (length, per, parts, tiles, count)),
        in_specs=[vmem, vmem, hbm],
        out_specs=hbm,
        out_shape=jax.ShapeDtypeStruct((length, width), f32),
        scratch_shapes=[pltpu.VMEM((length, width), f32)] * 2
        + [pltpu.SemaphoreType.DMA((1, count))] * 2,
        compiler_params=vmem_limit(20),
        name="gate",
    )(returned, query_short, skip)


def solution(mesh):
    sizes = (mesh.shape["ctx"], mesh.shape["tp"])
    return jax.shard_map(
        functools.partial(local, sizes),
        mesh=mesh,
        in_specs=(
            P(BOTH, None),
            P(BOTH, None),
            P(BOTH, None),
            P("ctx", "tp"),
            P(None, None, "tp"),
            P("tp"),
        ),
        out_specs=P(BOTH, None),
        check_vma=False,
    )
```

```python
import functools

import jax
import jax.numpy as jnp
import ml_dtypes
import numpy as np
from jax import lax
from jax.experimental import pallas as pl
from jax.experimental.pallas import tpu as pltpu
from jax.sharding import PartitionSpec as P

LANES = 128
PAD = 8
SPAN = 240.0
BOTH = ("ctx", "tp")
bf16, f32 = jnp.bfloat16, jnp.float32


def split_table(table, axis):
    high = table.astype(ml_dtypes.bfloat16)
    low = (table - high.astype(np.float64)).astype(ml_dtypes.bfloat16)
    parts = [high, low, high] if axis == 1 else [high, high, low]
    return np.concatenate(parts, axis)


@functools.lru_cache(maxsize=None)
def transform_tables(rows):
    m = np.arange(rows)
    k1 = np.arange(rows) + 0.5
    b = np.arange(LANES)
    outer = 2.0 * np.pi * np.outer(k1, m) / (2 * rows)
    inner = 2.0 * np.pi * (np.outer(b, b) % LANES) / LANES
    twist = 2.0 * np.pi * np.outer(k1, b) / (2 * LANES * rows)
    c, s = np.cos(inner), np.sin(inner)
    outer_forward = np.concatenate([np.cos(outer), -np.sin(outer)], 0)
    inner_forward = np.block([[c, -s], [s, c]])
    return (
        split_table(outer_forward, 1),
        split_table(inner_forward, 0),
        split_table(inner_forward.T, 0),
        split_table(outer_forward.T, 1),
        np.stack([np.cos(twist), -np.sin(twist)]).astype(np.float32),
    )


def halves(value):
    high = value.astype(bf16)
    return high, (value - high.astype(f32)).astype(bf16)


def from_left(table, value):
    high, low = halves(value)
    return jnp.dot(table[...], jnp.concatenate([high, high, low], 0), preferred_element_type=f32)


def from_right(value, table):
    high, low = halves(value)
    return jnp.dot(jnp.concatenate([high, low, high], 1), table[...], preferred_element_type=f32)


def forward(signal, rows, outer, inner, twist):
    group = signal.shape[1] // LANES
    columns = from_left(outer, signal)
    cos, sin = twist[0], twist[1]
    stacked = []
    for p in range(group):
        re = columns[:rows, p * LANES : (p + 1) * LANES]
        im = columns[rows:, p * LANES : (p + 1) * LANES]
        stacked.append(jnp.concatenate([re * cos - im * sin, re * sin + im * cos], 1))
    return from_right(jnp.concatenate(stacked, 0), inner)


def backward(spectrum, rows, inner, outer, twist):
    group = spectrum.shape[0] // rows
    lines = from_right(spectrum, inner)
    cos, sin = twist[0], twist[1]
    columns = []
    for p in range(group):
        re = lines[p * rows : (p + 1) * rows, :LANES]
        im = lines[p * rows : (p + 1) * rows, LANES:]
        columns.append(jnp.concatenate([re * cos + im * sin, im * cos - re * sin], 0))
    return from_left(outer, jnp.concatenate(columns, 1))


def encode(value, inverse_scale):
    magnitude = jnp.exp2(jnp.abs(value) * inverse_scale * SPAN - SPAN / 2)
    return jnp.where(value < 0, -magnitude, magnitude)


def decode(code, scale):
    magnitude = (jnp.log2(jnp.abs(code)) + SPAN / 2) * (scale * (1.0 / SPAN))
    return jnp.where(code < 0, -magnitude, magnitude)


def block_scale(largest):
    return jnp.maximum(largest * 1.0078125, 1e-30).astype(bf16).astype(f32)


def short_conv(ext_ref, weights, length):
    return (
        weights[0:1] * ext_ref[8 : 8 + length]
        + weights[1:2] * ext_ref[7 : 7 + length]
        + weights[2:3] * ext_ref[6 : 6 + length]
    )


def fill(ext_ref, current, before):
    ext_ref[6:8] = before
    ext_ref[8 : 8 + current.shape[0]] = current.astype(f32)


def columns(j):
    return pl.ds(pl.multiple_of(j * LANES, LANES), LANES)


def lane_index(shape):
    return lax.broadcasted_iota(jnp.int32, shape, 1)


def edges_kernel(q_ref, k_ref, v_ref, short_ref, skip_ref, edge_ref, own_ref, rows_ref):
    last = q_ref.shape[0]
    shard = own_ref.shape[1]
    rows_ref[...] = jnp.zeros_like(rows_ref)
    own_ref[0:6] = jnp.zeros((6, shard), f32)
    for i, ref in enumerate((q_ref, k_ref, v_ref)):
        rows_ref[2 * i : 2 * i + 2] = ref[...].astype(f32)[last - 2 : last]
        own_ref[6 + 3 * i : 9 + 3 * i] = short_ref[i]
    own_ref[15:16] = skip_ref[...]
    rest = own_ref[6:16]
    for i in range(3):
        part = rest.astype(bf16).astype(f32)
        rows_ref[6:16, i * shard : (i + 1) * shard] = part
        rest = rest - part
    edge_ref[...] = rows_ref[...].astype(bf16)


def taps_and_edge(idx_ref, refs, tiles, j):
    edge_ref, *held = refs
    depth = len(held) + 1
    behind = lax.rem(idx_ref[1] - j // tiles + depth, depth)
    tile = lax.rem(j, tiles)
    parts = [edge_ref[:, columns(tile + i * tiles)].astype(f32) for i in range(3)]
    taps = jnp.where(behind == 1, parts[0] + parts[1] + parts[2], held[0][:, columns(tile)])
    for s in range(2, depth):
        taps = jnp.where(behind == s, held[s - 1][:, columns(tile)], taps)
    first = (idx_ref[0] == 0) & (idx_ref[1] == 0)
    before = edge_ref[:, columns(j)].astype(f32)[0:6]
    return taps[6:15], taps[15:16], jnp.where(first, 0.0, before)


def column_copies(sources, targets, sems, j):
    return [
        pltpu.make_async_copy(s.at[:, columns(j)], t.at[:, columns(j)], sems.at[i, j])
        for i, (s, t) in enumerate(zip(sources, targets))
    ]


def start_all(copies_of, count):
    def step(j, carry):
        for copy in copies_of(j):
            copy.start()
        return carry

    lax.fori_loop(0, count, step, 0)


def wait_all(copies_of, count):
    def step(j, carry):
        for copy in copies_of(j):
            copy.wait()
        return carry

    lax.fori_loop(0, count, step, 0)


def rows_out_kernel(dims, idx_ref, k_ref, v_ref, *refs):
    length, per, parts, tiles, count = dims
    out_hbm, out_ref, k_ext, v_ext, out_sems = refs[-5:]
    aligned = per % 16 == 0
    steps = length // LANES

    def out_of(j):
        where = (pl.ds(lax.rem(j, tiles) * parts, parts), pl.ds(j // tiles, 1))
        return [pltpu.make_async_copy(out_ref.at[where], out_hbm.at[where], out_sems.at[j])]

    def tile(j, carry):
        weights, _, before = taps_and_edge(idx_ref, refs[:-5], tiles, j)
        fill(k_ext, k_ref[:, columns(j)], before[2:4])
        fill(v_ext, v_ref[:, columns(j)], before[4:6])
        mixed = short_conv(k_ext, weights[3:6], length) * short_conv(v_ext, weights[6:9], length)
        codes, scales = [], []
        for step in range(steps):
            block = mixed[step * LANES : (step + 1) * LANES]
            scale = block_scale(jnp.max(jnp.abs(block), 0, keepdims=True))
            scales.append(scale)
            code = encode(block, 1.0 / scale).astype(bf16).T
            codes.append(code if aligned else code.astype(f32))
        unused = [jnp.ones((PAD - steps, LANES), f32)]
        lines = jnp.concatenate([*scales, *unused], 0)
        for g in range(parts):
            place = out_ref.at[lax.rem(j, tiles) * parts + g, j // tiles]
            piece = [code[g * per : (g + 1) * per] for code in codes]
            line = pltpu.roll(lines, (-g * per) % LANES, 1)
            if aligned:
                for step in range(steps):
                    place[step * per : (step + 1) * per] = piece[step]
                place[steps * per :] = line.astype(bf16)
            else:
                place[...] = jnp.concatenate(piece + [line], 0).astype(bf16)
        for copy in out_of(j):
            copy.start()
        return carry

    lax.fori_loop(0, count, tile, 0)
    wait_all(out_of, count)


def gate_parts_kernel(dims, idx_ref, q_ref, k_ref, v_ref, *refs):
    length, tiles = dims
    short_ref, skip_ref, q_ext, k_ext, v_ext = refs[-5:]
    weights, bias, before = taps_and_edge(idx_ref, refs[:-5], tiles, pl.program_id(0))
    fill(q_ext, q_ref[...], before[0:2])
    fill(k_ext, k_ref[...], before[2:4])
    fill(v_ext, v_ref[...], before[4:6])
    mixed = short_conv(k_ext, weights[3:6], length) * short_conv(v_ext, weights[6:9], length)
    short_ref[...] = short_conv(q_ext, weights[0:3], length)
    skip_ref[...] = bias * mixed


def gate_kernel(dims, y_ref, short_ref, skip_hbm, out_hbm, skip_ref, out_ref, sems, out_sems):
    length, per, parts, tiles, count = dims
    steps = length // LANES
    rows = steps * per
    into = lambda j: column_copies((skip_hbm,), (skip_ref,), sems, j)
    out_of = lambda j: column_copies((out_ref,), (out_hbm,), out_sems, j)
    start_all(into, count)

    def tile(j, carry):
        pieces = [y_ref[lax.rem(j, tiles) * parts + g, j // tiles] for g in range(parts)]
        marks = [piece[rows:].astype(f32) for piece in pieces]
        if per % 16:
            pieces = [piece.astype(f32) for piece in pieces]
        lane = lane_index((PAD, LANES))
        moved = [pltpu.roll(marks[g], g * per, 1) for g in range(parts)]
        values = []
        for step in range(steps):
            code = jnp.concatenate([t[step * per : (step + 1) * per] for t in pieces], 0).T
            code = code.astype(f32)
            scale = jnp.ones((PAD, LANES), f32)
            for g in range(parts):
                inside = (lane >= g * per) & (lane < (g + 1) * per)
                scale = jnp.where(inside, moved[g], scale)
            values.append(decode(code, scale[step : step + 1]))
        for copy in into(j):
            copy.wait()
        for step in range(steps):
            here = pl.ds(step * LANES, LANES)
            out_ref[here, columns(j)] = short_ref[here, columns(j)] * (
                values[step] + skip_ref[here, columns(j)]
            )
        for copy in out_of(j):
            copy.start()
        return carry

    lax.fori_loop(0, count, tile, 0)
    wait_all(out_of, count)


def filter_rows_kernel(dims, idx_ref, h_ref, k_hbm, v_hbm, *refs):
    per, peers, chunk = dims
    outs, (k_ref, v_ref, turned, lines, sems) = refs[:peers], refs[peers:]
    fetches = [
        pltpu.make_async_copy(k_hbm, k_ref, sems.at[0]),
        pltpu.make_async_copy(v_hbm, v_ref, sems.at[1]),
    ]
    for fetch in fetches:
        fetch.start()
    me = idx_ref[0]
    parts = LANES // per
    for r in range(chunk):
        for c in range(h_ref.shape[1] // LANES):
            block = h_ref[r * LANES : (r + 1) * LANES, c * LANES : (c + 1) * LANES]
            scale = block_scale(jnp.max(jnp.abs(block), 0, keepdims=True))
            code = encode(block, 1.0 / scale).T.astype(bf16)
            wide = jnp.broadcast_to(scale, (PAD, LANES))
            for g in range(parts):
                turned[c * parts + g, r] = code[g * per : (g + 1) * per]
                lines[c * parts + g, r : r + 1] = pltpu.roll(wide, (-g * per) % LANES, 1)[0:1]
    for s in range(peers):
        peer = lax.bitwise_xor(me, s)
        outs[s][0 : chunk * per] = turned[peer].reshape(chunk * per, LANES)
        outs[s][chunk * per :] = lines[peer].astype(bf16)
    for fetch in fetches:
        fetch.wait()


def filter_kernel(dims, idx_ref, *refs):
    rows, per, peers, group = dims
    pieces = refs[:peers]
    outer, inner, twist, out_hbm, out_ref, coded, scales, held, wide, sems, out_sems = refs[peers:]
    me = idx_ref[0]
    chunk = rows // peers
    size = chunk * per
    copies = []
    for s in range(peers):
        peer = lax.bitwise_xor(me, s)
        copies.append(
            pltpu.make_async_copy(
                pieces[s].at[pl.ds(0, size)],
                coded.at[pl.ds(pl.multiple_of(peer * size, 16), size)],
                sems.at[0, s],
            )
        )
        copies.append(
            pltpu.make_async_copy(
                pieces[s].at[pl.ds(size, chunk)],
                scales.at[pl.ds(pl.multiple_of(peer * chunk, 16), chunk)],
                sems.at[1, s],
            )
        )
    for copy in copies:
        copy.start()
    for copy in copies:
        copy.wait()
    wide[...] = scales[...].astype(f32)

    def out_of(i):
        where = pl.ds(i * group, group)
        return [pltpu.make_async_copy(out_ref.at[where], out_hbm.at[where], out_sems.at[i])]

    def widen(i, carry):
        here = pl.ds(pl.multiple_of(i * size, 16), size)
        held[here, :] = coded[here, :].astype(f32)
        return carry

    lax.fori_loop(0, peers, widen, 0)

    def body(i):
        first = i * group
        near = pltpu.roll(wide[...], LANES - first, 1)
        signal = jnp.concatenate(
            [
                decode(held[pl.ds(first + p, rows, stride=per), :], near[:, p : p + 1])
                for p in range(group)
            ],
            1,
        )
        spectrum = forward(signal, rows, outer, inner, twist) * (1.0 / (LANES * rows))
        for p in range(group):
            out_ref[first + p] = spectrum[p * rows : (p + 1) * rows]
        for copy in out_of(i):
            copy.start()

    for i in range(per // group):
        body(i)
    wait_all(out_of, per // group)


def conv_kernel(
    dims, x_ref, h_hbm, outer, inner, inner_back, outer_back, twist, out_hbm, *scratch
):
    rows, per, lines, blocks, group, batch = dims
    held, h_ref, scales, found, out_ref, sems, out_sems = scratch
    steps = lines // per
    fetches = []
    for i in range(per // group):
        part = pl.ds(i * group, group)
        fetches.append(pltpu.make_async_copy(h_hbm.at[part], h_ref.at[part], sems.at[i]))
        fetches[-1].start()

    def unpack(i, carry):
        for j in range(batch):
            tile = x_ref[i * batch + j].astype(f32)
            held[pl.ds(pl.multiple_of((i * batch + j) * lines, 8), lines), :] = tile[:lines]
            scales[i * batch + j] = tile[lines : lines + steps]
        return carry

    lax.fori_loop(0, blocks // batch, unpack, 0)
    lane = lane_index((rows, LANES))

    def body(i):
        first = i * group
        near = pltpu.roll(scales[...].reshape(rows, LANES), LANES - first, 1)
        signal = jnp.concatenate(
            [
                decode(held[pl.ds(first + p, rows, stride=per), :], near[:, p : p + 1])
                for p in range(group)
            ],
            1,
        )
        spectrum = forward(signal, rows, outer, inner, twist)
        fetches[i].wait()
        joined = []
        for p in range(group):
            re = spectrum[p * rows : (p + 1) * rows, :LANES]
            im = spectrum[p * rows : (p + 1) * rows, LANES:]
            h_re, h_im = h_ref[first + p, :, :LANES], h_ref[first + p, :, LANES:]
            joined.append(jnp.concatenate([re * h_re - im * h_im, re * h_im + im * h_re], 1))
        result = backward(jnp.concatenate(joined, 0), rows, inner_back, outer_back, twist)
        for p in range(group):
            value = result[:, p * LANES : (p + 1) * LANES]
            scale = block_scale(jnp.max(jnp.abs(value), 1, keepdims=True))
            held[pl.ds(first + p, rows, stride=per), :] = encode(value, 1.0 / scale)
            found[...] = jnp.where(lane == first + p, scale, found[...])

    found[...] = jnp.ones_like(found)
    for i in range(per // group):
        body(i)
    scales[...] = found[...].reshape(scales.shape)

    def pack(i, carry):
        for j in range(batch):
            start = pl.multiple_of((i * batch + j) * lines, 8)
            line = jnp.concatenate([scales[i * batch + j], jnp.ones((PAD - steps, LANES), f32)], 0)
            tile = jnp.concatenate([held[pl.ds(start, lines), :], line], 0)
            out_ref[i * batch + j] = tile.astype(bf16)
        for copy in out_of(i):
            copy.start()
        return carry

    def out_of(i):
        part = pl.ds(i * batch, batch)
        return [pltpu.make_async_copy(out_ref.at[part], out_hbm.at[part], out_sems.at[i])]

    lax.fori_loop(0, blocks // batch, pack, 0)
    wait_all(out_of, blocks // batch)


def whole(array):
    return pl.BlockSpec(array.shape, lambda *_: (0,) * len(array.shape))


def vmem_limit(mebibytes):
    return pltpu.CompilerParams(vmem_limit_bytes=mebibytes * 1024 * 1024)


def local(sizes, query, key, value, long_filter, short_filter, skip_bias):
    peers, depth = sizes
    devices = peers * depth
    length, width = query.shape
    shard = long_filter.shape[1]
    per = shard // peers
    rows = length * devices // LANES
    lines = length // LANES * per
    parts = LANES // per
    tiles = shard // LANES
    group, batch = min(8, per), 8
    me = jnp.stack([lax.axis_index(axis) for axis in BOTH]).astype(jnp.int32)
    tables = transform_tables(rows)
    outer, inner, inner_back, outer_back, twist = (jnp.asarray(t) for t in tables)

    def crossed(array, axis, count):
        return [array[0]] + [
            lax.ppermute(array[s], axis, [(i, i ^ s) for i in range(count)])
            for s in range(1, count)
        ]

    query, key, value = (pltpu.with_memory_space_constraint(a, pltpu.HBM) for a in (query, key, value))
    last = pl.BlockSpec((16, width), lambda i: (length // 16 - 1, 0))
    taps_hbm, bias_hbm = (
        pltpu.with_memory_space_constraint(a, pltpu.HBM)
        for a in (short_filter, skip_bias.reshape(1, shard))
    )
    edge, own = pl.pallas_call(
        edges_kernel,
        grid=(1,),
        in_specs=[last] * 3 + [whole(short_filter), pl.BlockSpec((1, shard), lambda i: (0, 0))],
        out_specs=[
            pl.BlockSpec((16, width), lambda i: (0, 0)),
            pl.BlockSpec((16, shard), lambda i: (0, 0)),
        ],
        out_shape=[
            jax.ShapeDtypeStruct((16, width), bf16),
            jax.ShapeDtypeStruct((16, shard), f32),
        ],
        scratch_shapes=[pltpu.VMEM((16, width), f32)],
        compiler_params=vmem_limit(8),
        name="edges",
    )(query, key, value, taps_hbm, bias_hbm)

    def shifted(array, by):
        return lax.ppermute(array, BOTH, [(i, (i + by) % devices) for i in range(devices)])

    edge = shifted(edge, 1)
    taps = [own] + [shifted(own, s) for s in range(2, depth)]

    chunk = long_filter.shape[0] // LANES
    vmem, hbm = pl.BlockSpec(memory_space=pltpu.VMEM), pl.BlockSpec(memory_space=pltpu.HBM)
    *pieces, key_near, value_near = pl.pallas_call(
        functools.partial(filter_rows_kernel, (per, peers, chunk)),
        grid_spec=pltpu.PrefetchScalarGridSpec(
            num_scalar_prefetch=1,
            grid=(1,),
            in_specs=[whole(long_filter), hbm, hbm],
            out_specs=[pl.BlockSpec((chunk * per + chunk, LANES), lambda *_: (0, 0))] * peers
            + [vmem] * 2,
            scratch_shapes=[
                pltpu.VMEM((peers, chunk, per, LANES), bf16),
                pltpu.VMEM((peers, chunk, LANES), f32),
                pltpu.SemaphoreType.DMA((2,)),
            ],
        ),
        out_shape=[pltpu.HBM((chunk * per + chunk, LANES), bf16)] * peers
        + [pltpu.VMEM((length, width), bf16)] * 2,
        compiler_params=vmem_limit(16),
        name="filter_rows",
    )(me, long_filter, key, value)
    pieces = list(pieces)
    early = [s for s in (2, 4, 6) if s < peers]
    edge, *ready = lax.optimization_barrier((edge, *taps[1:], *(pieces[s] for s in early)))
    taps[1:] = ready[: depth - 2]
    for s, piece in zip(early, ready[depth - 2 :]):
        pieces[s] = piece
    pieces = crossed(pieces, "ctx", peers)

    row_spec = pl.BlockSpec((length, LANES), lambda j, _: (0, j))
    wire_shape = jax.ShapeDtypeStruct((peers, depth, lines + PAD, LANES), bf16)
    ext = pltpu.VMEM((length + 8, LANES), f32)
    count = width // LANES
    coded = pl.pallas_call(
        functools.partial(rows_out_kernel, (length, per, parts, tiles, count)),
        in_specs=[pl.BlockSpec(memory_space=pltpu.SMEM)] + [vmem] * (depth + 2),
        out_specs=hbm,
        out_shape=wire_shape,
        scratch_shapes=[
            pltpu.VMEM(wire_shape.shape, bf16),
            ext,
            ext,
            pltpu.SemaphoreType.DMA((count,)),
        ],
        compiler_params=vmem_limit(16),
        name="mixed_rows",
    )(me, key_near, value_near, edge, *taps)
    coded, *ready = lax.optimization_barrier((coded, *(pieces[s] for s in early)))
    for s, piece in zip(early, ready):
        pieces[s] = piece
    coded = coded.reshape(devices, lines + PAD, LANES)
    arrived = lax.all_to_all(coded, BOTH, split_axis=0, concat_axis=0, tiled=True)

    spectrum = pl.pallas_call(
        functools.partial(filter_kernel, (rows, per, peers, group)),
        grid_spec=pltpu.PrefetchScalarGridSpec(
            num_scalar_prefetch=1,
            grid=(1,),
            in_specs=[pl.BlockSpec(memory_space=pltpu.HBM)] * peers
            + [whole(outer), whole(inner), whole(twist)],
            out_specs=hbm,
            scratch_shapes=[
                pltpu.VMEM((per, rows, 2 * LANES), f32),
                pltpu.VMEM((rows * per, LANES), bf16),
                pltpu.VMEM((rows, LANES), bf16),
                pltpu.VMEM((rows * per, LANES), f32),
                pltpu.VMEM((rows, LANES), f32),
                pltpu.SemaphoreType.DMA((2, peers)),
                pltpu.SemaphoreType.DMA((per // group,)),
            ],
        ),
        out_shape=pltpu.HBM((per, rows, 2 * LANES), f32),
        compiler_params=vmem_limit(28),
        name="filter_spectrum",
    )(me, *pieces, outer, inner, twist)

    query_short, skip = pl.pallas_call(
        functools.partial(gate_parts_kernel, (length, tiles)),
        grid_spec=pltpu.PrefetchScalarGridSpec(
            num_scalar_prefetch=1,
            grid=(width // LANES,),
            in_specs=[row_spec] * 3 + [whole(edge)] + [whole(tap) for tap in taps],
            out_specs=[row_spec, row_spec],
            scratch_shapes=[ext] * 3,
        ),
        out_shape=[pltpu.VMEM((length, width), f32), pltpu.HBM((length, width), f32)],
        compiler_params=vmem_limit(12),
        name="gate_parts",
    )(me, query, key, value, edge, *taps)

    skip, spectrum = (pltpu.with_memory_space_constraint(a, pltpu.HBM) for a in (skip, spectrum))

    convolved = pl.pallas_call(
        functools.partial(conv_kernel, (rows, per, lines, devices, group, batch)),
        in_specs=[vmem, hbm] + [vmem] * 5,
        out_specs=hbm,
        out_shape=jax.ShapeDtypeStruct((devices, lines + PAD, LANES), bf16),
        scratch_shapes=[
            pltpu.VMEM((rows * per, LANES), f32),
            pltpu.VMEM((per, rows, 2 * LANES), f32),
            pltpu.VMEM((devices, length // LANES, LANES), f32),
            pltpu.VMEM((rows, LANES), f32),
            pltpu.VMEM((devices, lines + PAD, LANES), bf16),
            pltpu.SemaphoreType.DMA((per // group,)),
            pltpu.SemaphoreType.DMA((devices // batch,)),
        ],
        compiler_params=vmem_limit(28),
        name="long_conv",
    )(arrived, spectrum, outer, inner, inner_back, outer_back, twist)
    returned = lax.all_to_all(convolved, BOTH, split_axis=0, concat_axis=0, tiled=True)
    returned = returned.reshape(peers, depth, lines + PAD, LANES)

    return pl.pallas_call(
        functools.partial(gate_kernel, (length, per, parts, tiles, count)),
        in_specs=[vmem, vmem, hbm],
        out_specs=hbm,
        out_shape=jax.ShapeDtypeStruct((length, width), f32),
        scratch_shapes=[pltpu.VMEM((length, width), f32)] * 2
        + [pltpu.SemaphoreType.DMA((1, count))] * 2,
        compiler_params=vmem_limit(20),
        name="gate",
    )(returned, query_short, skip)


def solution(mesh):
    sizes = (mesh.shape["ctx"], mesh.shape["tp"])
    return jax.shard_map(
        functools.partial(local, sizes),
        mesh=mesh,
        in_specs=(
            P(BOTH, None),
            P(BOTH, None),
            P(BOTH, None),
            P("ctx", "tp"),
            P(None, None, "tp"),
            P("tp"),
        ),
        out_specs=P(BOTH, None),
        check_vma=False,
    )
```
